32 devices in a mesh: dp: 2 (over core), ctx: 4 (over y, x), seq: 4 (over z).
Axes of the slice: x: 2, y: 2, z: 4, core: 2. Of those that a mesh axis runs over, the one named last changes fastest.
Arguments:
- tokens: bfloat16 [2, 2048, 1536], P('dp', ('ctx', 'seq')), may hold values from -6 to 6
- cotangent: bfloat16 [2, 2048, 1536], P('dp', ('ctx', 'seq')), may hold values from -6 to 6
- in_weight: bfloat16 [1536, 6448], P(('dp', 'ctx')), may hold values from -0.15625 to 0.15625
- out_weight: bfloat16 [3072, 1536], P(('dp', 'ctx')), may hold values from -0.109375 to 0.109375
- vectors: bfloat16 [21392], P(('dp', 'ctx')), may hold values from -11 to 2, as said below
- in_moment: float32 [1536, 6448], P(('dp', 'ctx')), may hold values from -60 to 60
- in_square: float32 [1536, 6448], P(('dp', 'ctx')), may hold values from 100 to 2000
- out_moment: float32 [3072, 1536], P(('dp', 'ctx')), may hold values from -60 to 60
- out_square: float32 [3072, 1536], P(('dp', 'ctx')), may hold values from 100 to 2000
- vec_moment: float32 [21392], P(('dp', 'ctx')), may hold values from -60 to 60
- vec_square: float32 [21392], P(('dp', 'ctx')), may hold values from 100 to 2000
- step_count: int32 [1], replicated, may hold values from 1 to 20
Outputs:
- block_out: bfloat16 [2, 2048, 1536], P('dp', ('ctx', 'seq'))
- token_grad: float32 [2, 2048, 1536], P('dp', ('ctx', 'seq'))
- in_grad: float32 [1536, 6448], P(('dp', 'ctx'))
- new_in_moment: float32 [1536, 6448], P(('dp', 'ctx'))
- new_in_square: float32 [1536, 6448], P(('dp', 'ctx'))
- in_update: float32 [1536, 6448], P(('dp', 'ctx'))
- out_grad: float32 [3072, 1536], P(('dp', 'ctx'))
- new_out_moment: float32 [3072, 1536], P(('dp', 'ctx'))
- new_out_square: float32 [3072, 1536], P(('dp', 'ctx'))
- out_update: float32 [3072, 1536], P(('dp', 'ctx'))
- vec_grad: float32 [21392], P(('dp', 'ctx'))
- new_vec_moment: float32 [21392], P(('dp', 'ctx'))
- new_vec_square: float32 [21392], P(('dp', 'ctx'))
- vec_update: float32 [21392], P(('dp', 'ctx'))
The draws below stay inside these ranges and needn't reach their ends.
Inputs may be any that keep to these rules, and one draw needn't show every extreme that they name: vectors' gains and skip weights lie in 0.5 to 1.5; dt_bias is the inverse softplus of a per-head step size.
All inputs are finite; a program needn't handle non-finite values.
Results may differ from the reference program's by a relative error of at most 0.0085.
Values may be sent and summed in bfloat16 or wider, within the bound.
No kernel may reach another device: no remote copies, remote signals or barrier semaphores. Data moves between devices by JAX's collectives and lax.ppermute only.
A program may use at most 320 MiB of HBM per device.

```python
import math
from functools import partial
import jax
import jax.numpy as jnp
from jax import lax

D = 1536
HEADS = 48
HEADDIM = 64
STATE = 128
CONV = 4
SPAN = 256
DI = 3072
EPROJ = 6448
VEC = 21392
SEQS = 2
LEN = 2048


def draw_vectors(key, part):
    inner_width = HEADS * HEADDIM
    channels = inner_width + 2 * STATE
    keys_list = jax.random.split(key, 7)
    gain_in = jax.random.uniform(keys_list[0], (D,), jnp.float32, 0.5, 1.5)
    conv_weight = jnp.clip(0.5 * jax.random.normal(keys_list[1], (CONV * channels,), jnp.float32), -2.0, 2.0)
    conv_bias = jax.random.uniform(keys_list[2], (channels,), jnp.float32, -0.5, 0.5)
    gain_out = jax.random.uniform(keys_list[3], (inner_width,), jnp.float32, 0.5, 1.5)
    low_end = math.log(0.5 / LEN)
    high_end = math.log(0.04)
    step_size = jnp.exp(jax.random.uniform(keys_list[4], (HEADS,), jnp.float32, low_end, high_end))
    dt_bias = jnp.log(jnp.expm1(step_size))
    a_log = jax.random.uniform(keys_list[5], (HEADS,), jnp.float32, -0.5, 0.5)
    d_skip = jax.random.uniform(keys_list[6], (HEADS,), jnp.float32, 0.5, 1.5)
    return jnp.concatenate([gain_in, conv_weight, conv_bias, gain_out, dt_bias, a_log, d_skip]).astype(jnp.bfloat16)


def level_of(key, extent, shards, smallest, high):
    loudness = 1.0
    for dim, parts in shards:
        steps = jax.random.uniform(jax.random.fold_in(jax.random.fold_in(key, 6), dim), (parts,), jnp.float32, smallest / len(shards), high / len(shards))
        loudness = loudness * jnp.repeat(jnp.exp(steps), extent[dim] // parts).reshape((-1,) + (1,) * (len(extent) - 1 - dim))
    return loudness


def noise(rng, extent, width, limit, cuts=(), dtype=jnp.bfloat16):
    loudness = level_of(rng, extent, cuts, -0.22, 0.18) if cuts else 1.0
    entries = jax.random.normal(rng, extent, jnp.float32) * width * loudness
    return jnp.minimum(jnp.maximum(entries, -limit), limit).astype(dtype)


def setup_inputs(seed: int = 0) -> dict:
    key_of = jax.random.split(jax.random.key(seed), 13)
    tokens = noise(key_of[0], (SEQS, LEN, D), 1.0, 6.0, ((0, 2), (1, 16)))
    cotangent = noise(key_of[1], (SEQS, LEN, D), 1.0, 6.0, ((0, 2), (1, 16)))
    in_weight = noise(key_of[2], (D, EPROJ), D ** -0.5, 0.15625, ((0, 8),))
    out_weight = noise(key_of[3], (DI, D), DI ** -0.5, 0.109375, ((0, 8),))
    vectors = draw_vectors(jax.random.fold_in(key_of[12], 71), 0)
    in_moment = noise(key_of[5], (D, EPROJ), 10.0, 60.0, ((0, 8),), jnp.float32)
    in_square = jnp.clip(jnp.exp(math.log(2000.0) - 2.9957323 * jax.random.uniform(key_of[6], (D, EPROJ), jnp.float32) ** level_of(key_of[6], (D, EPROJ), ((0, 8),), -0.2, 0.2)), 100.0, 2000.0)
    out_moment = noise(key_of[7], (DI, D), 10.0, 60.0, ((0, 8),), jnp.float32)
    out_square = jnp.clip(jnp.exp(math.log(2000.0) - 2.9957323 * jax.random.uniform(key_of[8], (DI, D), jnp.float32) ** level_of(key_of[8], (DI, D), ((0, 8),), -0.2, 0.2)), 100.0, 2000.0)
    vec_moment = noise(key_of[9], (VEC,), 10.0, 60.0, ((0, 8),), jnp.float32)
    vec_square = jnp.clip(jnp.exp(math.log(2000.0) - 2.9957323 * jax.random.uniform(key_of[10], (VEC,), jnp.float32) ** level_of(key_of[10], (VEC,), ((0, 8),), -0.2, 0.2)), 100.0, 2000.0)
    step_count = jax.random.randint(key_of[11], (1,), 1, 21).astype(jnp.int32)
    return {"tokens": tokens, "cotangent": cotangent, "in_weight": in_weight, "out_weight": out_weight, "vectors": vectors, "in_moment": in_moment, "in_square": in_square, "out_moment": out_moment, "out_square": out_square, "vec_moment": vec_moment, "vec_square": vec_square, "step_count": step_count}


@jax.custom_vjp
def low(v):
    return lax.optimization_barrier(v.astype(jnp.bfloat16)).astype(jnp.float32)

@jax.custom_vjp
def low_back(v):
    return v

def low_keep(v):
    return (low(v), None)

def low_pass(kept, grad):
    return (grad,)

def back_keep(v):
    return (v, None)

def back_low(kept, grad):
    return (low(grad),)
low.defvjp(low_keep, low_pass)
low_back.defvjp(back_keep, back_low)
highest = lax.Precision.HIGHEST
eps_norm = 1e-05
beta_one = 0.9
beta_two = 0.95
adam_eps = 1e-08
decay_rate = 0.1
learn_rate = 0.02

def unpack(vector):
    inner_width = HEADS * HEADDIM
    channels = inner_width + 2 * STATE
    offset = 0
    gain_in = vector[offset:offset + D]
    offset += D
    conv_weight = vector[offset:offset + CONV * channels].reshape(CONV, channels)
    offset += CONV * channels
    conv_bias = vector[offset:offset + channels]
    offset += channels
    gain_out = vector[offset:offset + inner_width]
    offset += inner_width
    dt_bias = vector[offset:offset + HEADS]
    offset += HEADS
    a_log = vector[offset:offset + HEADS]
    offset += HEADS
    d_skip = vector[offset:offset + HEADS]
    return (gain_in, conv_weight, conv_bias, gain_out, dt_bias, a_log, d_skip)

def rms_scale(values):
    return lax.rsqrt(lax.optimization_barrier(jnp.mean(values * values, axis=-1, keepdims=True)) + eps_norm)

def intra_span(values, step_sizes, in_keys, out_keys, cumulative):
    row_count = values.shape[0]
    key_inner = jnp.dot(out_keys, in_keys.T, precision=highest)
    positions = jnp.arange(row_count)
    causal = (positions[:, None] >= positions[None, :])[:, :, None]
    log_gap = cumulative[:, None, :] - cumulative[None, :, :]
    weights = jnp.where(causal, jnp.exp(jnp.where(causal, log_gap, 0.0)), 0.0) * key_inner[:, :, None]
    scaled = values * step_sizes[:, :, None]
    return (jnp.einsum('qkh,khp->qhp', weights, scaled, precision=highest), scaled)

def span_state(carry_state, scaled, in_keys, cumulative):
    to_end = jnp.exp(cumulative[-1:, :] - cumulative)
    fresh = jnp.einsum('kh,khp,kn->hpn', to_end, scaled, in_keys, precision=highest)
    return carry_state * jnp.exp(cumulative[-1])[:, None, None] + fresh

def ref_span(carry_state, pieces, a_rate):
    values, step_sizes, in_keys, out_keys = pieces
    cumulative = jnp.cumsum(step_sizes * a_rate, axis=0)
    within, scaled = intra_span(values, step_sizes, in_keys, out_keys, cumulative)
    across = jnp.einsum('qn,hpn->qhp', out_keys, carry_state, precision=highest) * jnp.exp(cumulative)[:, :, None]
    return (span_state(carry_state, scaled, in_keys, cumulative), within + across)

def forward(tokens, in_weight, out_weight, vector):
    gain_in, conv_weight, conv_bias, gain_out, dt_bias, a_log, d_skip = unpack(vector)
    inner_width = HEADS * HEADDIM
    channels = inner_width + 2 * STATE
    length = tokens.shape[0]
    normed = low(tokens * rms_scale(tokens) * gain_in)
    projected = low_back(low(jnp.dot(normed, in_weight, precision=highest)))
    gate_part = projected[:, :inner_width]
    mixed_in = projected[:, inner_width:inner_width + channels]
    step_raw = low_back(projected[:, inner_width + channels:])
    padded = jnp.concatenate([jnp.zeros((CONV - 1, channels), jnp.float32), mixed_in], axis=0)
    conv_sum = conv_bias + sum((conv_weight[lag_index] * padded[lag_index:lag_index + length] for lag_index in range(CONV)))
    activated = jax.nn.silu(conv_sum)
    values = low(activated[:, :inner_width]).reshape(length, HEADS, HEADDIM)
    in_keys = low(activated[:, inner_width:inner_width + STATE])
    out_keys = low(activated[:, inner_width + STATE:])
    step_sizes = jax.nn.softplus(step_raw + dt_bias)
    a_rate = -jnp.exp(a_log)
    span_count = length // SPAN
    pieces = (values.reshape(span_count, SPAN, HEADS, HEADDIM), step_sizes.reshape(span_count, SPAN, HEADS), in_keys.reshape(span_count, SPAN, STATE), out_keys.reshape(span_count, SPAN, STATE))
    start_state = jnp.zeros((HEADS, HEADDIM, STATE), jnp.float32)
    final_state, outputs = lax.scan(jax.checkpoint(partial(ref_span, a_rate=a_rate)), start_state, pieces)
    scan_out = outputs.reshape(length, HEADS, HEADDIM) + d_skip[:, None] * values
    mixed_out = low_back(low(scan_out.reshape(length, inner_width)))
    gated_out = mixed_out * jax.nn.silu(gate_part)
    normed_out = low(gated_out * rms_scale(gated_out) * gain_out)
    return tokens + jnp.dot(normed_out, out_weight, precision=highest)

def adam_update(weight, grad, moment, square, step_count):
    step_float = step_count[0].astype(jnp.float32)
    new_moment = beta_one * moment + (1.0 - beta_one) * grad
    new_square = beta_two * square + (1.0 - beta_two) * grad * grad
    corr_one = 1.0 - jnp.power(jnp.float32(beta_one), step_float)
    corr_two = 1.0 - jnp.power(jnp.float32(beta_two), step_float)
    update = -learn_rate * (new_moment / corr_one / (jnp.sqrt(new_square / corr_two) + adam_eps) + decay_rate * weight)
    return (grad, new_moment, new_square, update)

def reference(tokens, cotangent, in_weight, out_weight, vectors, in_moment, in_square, out_moment, out_square, vec_moment, vec_square, step_count):
    weights = (in_weight.astype(jnp.float32), out_weight.astype(jnp.float32), vectors.astype(jnp.float32))

    def one_sequence(totals, pair):
        seq_tokens, seq_cot = pair
        result, pullback = jax.vjp(forward, seq_tokens.astype(jnp.float32), weights[0], weights[1], weights[2])
        grad_list = pullback(seq_cot.astype(jnp.float32))
        totals = (totals[0] + grad_list[1], totals[1] + grad_list[2], totals[2] + grad_list[3])
        return (totals, (result.astype(jnp.bfloat16), grad_list[0]))
    zero_grads = (jnp.zeros_like(weights[0]), jnp.zeros_like(weights[1]), jnp.zeros_like(weights[2]))
    totals, outputs = lax.scan(one_sequence, zero_grads, (tokens, cotangent))
    block_out, token_grad = outputs
    in_out = adam_update(weights[0], totals[0], in_moment, in_square, step_count)
    out_out = adam_update(weights[1], totals[1], out_moment, out_square, step_count)
    vec_out = adam_update(weights[2], totals[2], vec_moment, vec_square, step_count)
    return (block_out, token_grad, in_out[0], in_out[1], in_out[2], in_out[3], out_out[0], out_out[1], out_out[2], out_out[3], vec_out[0], vec_out[1], vec_out[2], vec_out[3])
```

```python
import functools

import jax
import jax.numpy as jnp
from jax import lax
from jax.experimental import pallas as pl
from jax.experimental.pallas import tpu as pltpu
from jax.sharding import PartitionSpec as P

D = 1536
HEADS = 48
HEADDIM = 64
STATE = 128
CONV = 4
CHUNK = 128
LANES = 128
INNER = HEADS * HEADDIM
CHANNELS = INNER + 2 * STATE

highest = lax.Precision.HIGHEST
eps_norm = 1e-05
beta_one = 0.9
beta_two = 0.95
adam_eps = 1e-08
decay_rate = 0.1
learn_rate = 0.02
bf16 = jnp.bfloat16
f32 = jnp.float32
PLANE = ("dp", "ctx")
WORLD = ("dp", "ctx", "seq")


def shift_pairs(n, by):
    return [(i, i + by) for i in range(n) if 0 <= i + by < n]


def flip_pairs(n, bit):
    return [(i, i ^ bit) for i in range(n)]


def manual():
    return lax.axis_size("seq") == 4 and lax.axis_size("ctx") == 4 and lax.axis_size("dp") == 2


def gather_seq_blocks(x):
    n, me = lax.axis_size("seq"), lax.axis_index("seq")
    right, left = [x], [x]
    for k in range(1, n):
        right.append(lax.ppermute(right[-1], "seq", [(i, i + 1) for i in range(k - 1, n - 1)]))
        left.append(lax.ppermute(left[-1], "seq", [(i, i - 1) for i in range(1, n - k + 1)]))
    return [x] + [jnp.where(me >= k, right[k], left[n - k]) for k in range(1, n)]


def gather_seq(x):
    n, me = lax.axis_size("seq"), lax.axis_index("seq")
    if not manual():
        return lax.all_gather(x, "seq", axis=0, tiled=True)
    rows = x.shape[0]
    out = jnp.zeros((n * rows, x.shape[1]), x.dtype)
    for k, block in enumerate(gather_seq_blocks(x)):
        out = lax.dynamic_update_slice_in_dim(out, block, lax.rem(me - k + n, n) * rows, 0)
    return out


def scatter_seq(x):
    n, me = lax.axis_size("seq"), lax.axis_index("seq")
    rows = x.shape[0] // n
    if not manual():
        return lax.psum_scatter(x.astype(bf16), "seq", scatter_dimension=0, tiled=True).astype(f32)

    def piece(block):
        return lax.dynamic_slice_in_dim(x, jnp.clip(block, 0, n - 1) * rows, rows, 0).astype(f32)

    total = piece(me)
    right = left = None
    for t in range(1, n):
        send = piece(me + n - t) if right is None else piece(me + n - t) + right
        right = lax.ppermute(send.astype(bf16), "seq", [(i, i + 1) for i in range(t)]).astype(f32)
        send = piece(me + t - n) if left is None else piece(me + t - n) + left
        left = lax.ppermute(
            send.astype(bf16), "seq", [(n - 1 - i, n - 2 - i) for i in range(t)]
        ).astype(f32)
    return total + right + left


def gather_plane(x):
    if not manual():
        return lax.all_gather(x, PLANE, axis=0, tiled=True)
    rows = x.shape[0]
    me_d, me_c = lax.axis_index("dp"), lax.axis_index("ctx")
    across = lax.ppermute(x, "ctx", flip_pairs(4, 1))
    along = lax.ppermute(x, "ctx", flip_pairs(4, 2))
    half = rows // 2
    upper = lax.ppermute(along[:half], "ctx", flip_pairs(4, 1))
    lower = lax.ppermute(across[half:], "ctx", flip_pairs(4, 2))
    parts = [x, across, along, jnp.concatenate([upper, lower], axis=0)]
    out = jnp.zeros((8 * rows, x.shape[1]), x.dtype)
    for c, part in enumerate(parts):
        other = lax.ppermute(part, "dp", [(0, 1), (1, 0)])
        for d, block in ((0, part), (1, other)):
            place = (me_d ^ d) * 4 + (me_c ^ c)
            out = lax.dynamic_update_slice_in_dim(out, block, place * rows, 0)
    return out


def gather_plane_small(x):
    if not manual():
        return lax.all_gather(x, PLANE, axis=0, tiled=True)
    rows = x.shape[0]
    me_d, me_c = lax.axis_index("dp"), lax.axis_index("ctx")
    across = lax.ppermute(x, "ctx", flip_pairs(4, 1))
    both = jnp.concatenate([x, across], axis=0)
    four = jnp.concatenate([both, lax.ppermute(both, "ctx", flip_pairs(4, 2))], axis=0)
    other = lax.ppermute(four, "dp", [(0, 1), (1, 0)])
    out = jnp.zeros((8 * rows, x.shape[1]), x.dtype)
    for d, block in ((0, four), (1, other)):
        for c in range(4):
            place = (me_d ^ d) * 4 + (me_c ^ c)
            out = lax.dynamic_update_slice_in_dim(
                out, block[c * rows : (c + 1) * rows], place * rows, 0
            )
    return out


def scatter_plane(x):
    if not manual():
        return lax.psum_scatter(x.astype(bf16), PLANE, scatter_dimension=0, tiled=True).astype(f32)
    rows = x.shape[0] // 8
    me_d, me_c = lax.axis_index("dp"), lax.axis_index("ctx")
    mine = lax.dynamic_slice_in_dim(x, me_d * 4 * rows, 4 * rows, 0)
    yours = lax.dynamic_slice_in_dim(x, (1 - me_d) * 4 * rows, 4 * rows, 0)
    got = lax.ppermute(yours.astype(bf16), "dp", [(0, 1), (1, 0)])
    chip = mine.astype(f32) + got.astype(f32)
    total = lax.dynamic_slice_in_dim(chip, me_c * rows, rows, 0)
    for bit in (1, 2, 3):
        send = lax.dynamic_slice_in_dim(chip, (me_c ^ bit) * rows, rows, 0).astype(bf16)
        total = total + lax.ppermute(send, "ctx", flip_pairs(4, bit)).astype(f32)
    return total


def gather_out_rows(x, width):
    sidx = lax.axis_index("seq")
    if not manual():
        full = lax.all_gather(x, PLANE, axis=0, tiled=True)
        return lax.dynamic_slice_in_dim(full, sidx * width, width, 0)
    me_d, me_c = lax.axis_index("dp"), lax.axis_index("ctx")

    def flat(d, c, s):
        return (d * 4 + c) * 4 + s

    first, second, third, fourth = [], [], [], []
    for s in range(4):
        d, y = s // 2, s % 2
        for h in range(2):
            first.append((flat(d, 2 * y + h, s), flat(d, 2 * y + 1 - h, s)))
            second.append((flat(d, 2 * y + h, s), flat(d, 2 * (1 - y) + h, s)))
            third.append((flat(d, 2 * (1 - y) + h, s), flat(d, 2 * (1 - y) + 1 - h, s)))
        for c in range(4):
            fourth.append((flat(d, c, s), flat(1 - d, c, s)))
    beside = lax.ppermute(x, WORLD, first)
    along = lax.ppermute(x, WORLD, second)
    beyond = lax.ppermute(along, WORLD, third)
    source = (me_d == sidx // 2) & (me_c // 2 == lax.rem(sidx, 2))
    mine = jnp.where(source, x, along)
    other = jnp.where(source, beside, beyond)
    low = lax.rem(me_c, 2) == 0
    rows = jnp.concatenate([jnp.where(low, mine, other), jnp.where(low, other, mine)], axis=0)
    back = lax.ppermute(rows, WORLD, fourth)
    return jnp.where(me_d == sidx // 2, rows, back)


def exchange(x, axis):
    n = lax.axis_size(axis)
    if not manual():
        return lax.psum(x, axis)
    bit = 1
    while bit < n:
        x = x + lax.ppermute(x, axis, flip_pairs(n, bit))
        bit *= 2
    return x


def dot_nn(a, b, precision=None):
    return lax.dot_general(
        a, b, (((1,), (0,)), ((), ())), precision=precision, preferred_element_type=f32
    )


def dot_nt(a, b):
    return lax.dot_general(a, b, (((1,), (1,)), ((), ())), preferred_element_type=f32)


def dot_tn(a, b):
    return lax.dot_general(a, b, (((0,), (0,)), ((), ())), preferred_element_type=f32)


def low_lanes(rows):
    return lax.broadcasted_iota(jnp.int32, (rows, LANES), 1) < HEADDIM


def spread(x, pair, low):
    rows = x.shape[0]
    first = jnp.broadcast_to(x[:, 2 * pair : 2 * pair + 1], (rows, LANES))
    second = jnp.broadcast_to(x[:, 2 * pair + 1 : 2 * pair + 2], (rows, LANES))
    return jnp.where(low, first, second)


def spread_all(x, pairs, low):
    return jnp.concatenate([spread(x, j, low) for j in range(pairs)], axis=1)


def softplus(x):
    tail = jnp.exp(-jnp.abs(x))
    one = 1.0 + tail
    rest = one - 1.0
    return jnp.maximum(x, 0.0) + jnp.where(
        rest == 0.0, tail, jnp.log(one) * tail / jnp.where(rest == 0.0, 1.0, rest)
    )


def pack_state(pk_ref, state, log_row, pairs, low_row):
    pk_ref[0:STATE, :] = state.astype(bf16)
    total = spread_all(log_row, pairs, low_row)
    high = total.astype(bf16)
    rest = total - high.astype(f32)
    mid = rest.astype(bf16)
    last = (rest - mid.astype(f32)).astype(bf16)
    width = total.shape[1]
    row = lax.broadcasted_iota(jnp.int32, (16, width), 0)
    zero = jnp.zeros((16, width), f32)
    tail = jnp.where(row == 0, high.astype(f32), zero)
    tail = jnp.where(row == 1, mid.astype(f32), tail)
    tail = jnp.where(row == 2, last.astype(f32), tail)
    pk_ref[STATE : STATE + 16, :] = tail.astype(bf16)


def states_kernel(pairs, chunks, raw_ref, hp_ref, v_ref, k_ref, dt_ref, cum_ref, sc_ref, pk_ref, st):
    rate = -jnp.exp(hp_ref[1:2, :])
    bias = hp_ref[0:1, :]
    rows_i = lax.broadcasted_iota(jnp.int32, (CHUNK, CHUNK), 0)
    cols_i = lax.broadcasted_iota(jnp.int32, (CHUNK, CHUNK), 1)
    tri = jnp.where(rows_i >= cols_i, 1.0, 0.0).astype(f32)
    low, low_row = low_lanes(CHUNK), low_lanes(1)
    st[...] = jnp.zeros_like(st)

    def chunk(c, total):
        rows = pl.ds(pl.multiple_of(c * CHUNK, CHUNK), CHUNK)
        dt = softplus(raw_ref[rows, :].astype(f32) + bias)
        cum = dot_nn(tri, dt * rate, highest)
        dt_ref[rows, :] = dt
        cum_ref[rows, :] = cum
        state = st[...]
        sc_ref[c] = state
        end = cum[CHUNK - 1 : CHUNK, :]
        weight = jnp.exp(end - cum) * dt
        scaled = jnp.concatenate(
            [
                (spread(weight, j, low) * v_ref[rows, j * LANES : (j + 1) * LANES].astype(f32)).astype(bf16)
                for j in range(pairs)
            ],
            axis=1,
        )
        fresh = dot_tn(k_ref[rows, 0:STATE], scaled)
        st[...] = jnp.exp(spread_all(end, pairs, low_row)) * state + fresh
        return total + end

    total = lax.fori_loop(0, chunks, chunk, jnp.zeros((1, LANES), f32))
    pack_state(pk_ref, st[...], total, pairs, low_row)


def decay_matrix(cum, cum_t, head, causal):
    gap = cum[:, head : head + 1] - cum_t[head : head + 1, :]
    return jnp.where(causal, jnp.exp(jnp.minimum(gap, 0.0)), 0.0)


def stacked(u, low):
    zero = jnp.zeros_like(u)
    return jnp.concatenate([jnp.where(low, u, zero), jnp.where(low, zero, u)], axis=0)


def outputs_kernel(pairs, chunks, v_ref, k_ref, dt_ref, cum_ref, sc_ref, sin_ref, hp_ref, y_ref):
    rows_i = lax.broadcasted_iota(jnp.int32, (CHUNK, CHUNK), 0)
    cols_i = lax.broadcasted_iota(jnp.int32, (CHUNK, CHUNK), 1)
    causal = rows_i >= cols_i
    low, low_row = low_lanes(CHUNK), low_lanes(1)

    def chunk(c, offset):
        rows = pl.ds(pl.multiple_of(c * CHUNK, CHUNK), CHUNK)
        dt, cum = dt_ref[rows, :], cum_ref[rows, :]
        cum_t = cum.T
        grown = jnp.exp(cum)
        in_keys, out_keys = k_ref[rows, 0:STATE], k_ref[rows, STATE : 2 * STATE]
        inner = dot_nt(out_keys, in_keys)
        start = sc_ref[c] + jnp.exp(spread_all(offset, pairs, low_row)) * sin_ref[...]
        carried = dot_nn(out_keys, start.astype(bf16))
        for j in range(pairs):
            lanes = slice(j * LANES, (j + 1) * LANES)
            v = v_ref[rows, lanes].astype(f32)
            u = (spread(dt, j, low) * v).astype(bf16)
            weights = jnp.concatenate(
                [(decay_matrix(cum, cum_t, 2 * j + i, causal) * inner).astype(bf16) for i in (0, 1)], axis=1
            )
            y = dot_nn(weights, stacked(u, low))
            y = y + spread(grown, j, low) * carried[:, lanes]
            y = y + spread(hp_ref[2:3, :], j, low_row) * v
            y_ref[rows, lanes] = y.astype(bf16)
        return offset + cum[CHUNK - 1 : CHUNK, :]

    lax.fori_loop(0, chunks, chunk, jnp.zeros((1, LANES), f32))


def direct_kernel(pairs, chunks, dy_ref, k_ref, cum_ref, pk_ref, st):
    low, low_row = low_lanes(CHUNK), low_lanes(1)
    st[...] = jnp.zeros_like(st)

    def chunk(i, total):
        c = chunks - 1 - i
        rows = pl.ds(pl.multiple_of(c * CHUNK, CHUNK), CHUNK)
        cum = cum_ref[rows, :]
        end = cum[CHUNK - 1 : CHUNK, :]
        grown = jnp.exp(cum)
        scaled = jnp.concatenate(
            [
                (spread(grown, j, low) * dy_ref[rows, j * LANES : (j + 1) * LANES].astype(f32)).astype(bf16)
                for j in range(pairs)
            ],
            axis=1,
        )
        fresh = dot_tn(k_ref[rows, STATE : 2 * STATE], scaled)
        st[...] = jnp.exp(spread_all(end, pairs, low_row)) * st[...] + fresh
        return total + end

    total = lax.fori_loop(0, chunks, chunk, jnp.zeros((1, LANES), f32))
    pack_state(pk_ref, st[...], total, pairs, low_row)


def split_dot(x, sel):
    high = x.astype(bf16)
    rest = (x - high.astype(f32)).astype(bf16)
    return dot_nn(high, sel) + dot_nn(rest, sel)


def back_kernel(
    pairs, chunks, v_ref, dy_ref, k_ref, raw_ref, dt_ref, cum_ref, sc_ref, sin_ref, sg_ref, hp_ref,
    gv_ref, gk_ref, graw_ref, gh_ref, st, offs, x_buf,
):
    rate = -jnp.exp(hp_ref[1:2, :])
    bias = hp_ref[0:1, :]
    rows_i = lax.broadcasted_iota(jnp.int32, (CHUNK, CHUNK), 0)
    cols_i = lax.broadcasted_iota(jnp.int32, (CHUNK, CHUNK), 1)
    causal, causal_t = rows_i >= cols_i, cols_i >= rows_i
    tri_t = jnp.where(causal_t, 1.0, 0.0).astype(f32)
    low, low_row = low_lanes(CHUNK), low_lanes(1)
    width = pairs * LANES
    lane_i = lax.broadcasted_iota(jnp.int32, (width, LANES), 0)
    head_i = lax.broadcasted_iota(jnp.int32, (width, LANES), 1)
    owner = (lane_i >= head_i * HEADDIM) & (lane_i < (head_i + 1) * HEADDIM)
    sel = jnp.where(owner, 1.0, 0.0).astype(bf16)
    st[...] = sg_ref[...]
    gh_ref[...] = jnp.zeros_like(gh_ref)

    def mark(c, offset):
        offs[pl.ds(c, 1), :] = offset
        last = cum_ref[pl.ds(c * CHUNK + CHUNK - 1, 1), :]
        return offset + last

    lax.fori_loop(0, chunks, mark, jnp.zeros((1, LANES), f32))

    def chunk(i, skip):
        c = chunks - 1 - i
        rows = pl.ds(pl.multiple_of(c * CHUNK, CHUNK), CHUNK)
        dt, cum = dt_ref[rows, :], cum_ref[rows, :]
        cum_t = cum.T
        end = cum[CHUNK - 1 : CHUNK, :]
        grown = jnp.exp(cum)
        fading = jnp.exp(end - cum)
        in_keys, out_keys = k_ref[rows, 0:STATE], k_ref[rows, STATE : 2 * STATE]
        inner = dot_nt(out_keys, in_keys)
        inner_t = dot_nt(in_keys, out_keys)
        start = sc_ref[c] + jnp.exp(spread_all(offs[pl.ds(c, 1), :], pairs, low_row)) * sin_ref[...]
        start_low = start.astype(bf16)
        later = st[...]
        later_low = later.astype(bf16)
        carried = dot_nn(out_keys, start_low)
        passed = dot_nn(in_keys, later_low)
        grad_inner = jnp.zeros((CHUNK, CHUNK), f32)
        grown_dy, fading_u, after, skips = [], [], [], []
        for j in range(pairs):
            lanes = slice(j * LANES, (j + 1) * LANES)
            v = v_ref[rows, lanes].astype(f32)
            dy_low = dy_ref[rows, lanes]
            dy = dy_low.astype(f32)
            dt_j, grown_j, fading_j = spread(dt, j, low), spread(grown, j, low), spread(fading, j, low)
            u_low = (dt_j * v).astype(bf16)
            u = u_low.astype(f32)
            u_two = stacked(u_low, low)
            decays = [decay_matrix(cum, cum_t, 2 * j + i, causal) for i in (0, 1)]
            weights = jnp.concatenate([(decay * inner).astype(bf16) for decay in decays], axis=1)
            weights_t = jnp.concatenate(
                [
                    (
                        jnp.where(
                            causal_t,
                            jnp.exp(
                                jnp.minimum(
                                    cum_t[2 * j + i : 2 * j + i + 1, :] - cum[:, 2 * j + i : 2 * j + i + 1], 0.0
                                )
                            ),
                            0.0,
                        )
                        * inner_t
                    ).astype(bf16)
                    for i in (0, 1)
                ],
                axis=1,
            )
            y = dot_nn(weights, u_two) + grown_j * carried[:, lanes]
            du_in = dot_nn(weights_t, stacked(dy_low, low))
            du_out = fading_j * passed[:, lanes]
            du = du_in + du_out
            grad_two = dot_nt(dy_low, u_two)
            grad_inner = grad_inner + decays[0] * grad_two[:, :CHUNK] + decays[1] * grad_two[:, CHUNK:]
            x_buf[0:CHUNK, lanes] = dy * y - u * du
            x_buf[CHUNK : 2 * CHUNK, lanes] = v * du
            after.append(jnp.sum(u * du_out, axis=0, keepdims=True))
            skips.append(jnp.sum(dy * v, axis=0, keepdims=True))
            grown_dy.append((grown_j * dy).astype(bf16))
            fading_u.append((fading_j * u).astype(bf16))
            gv_ref[rows, lanes] = dt_j * du + spread(hp_ref[2:3, :], j, low_row) * dy
        grown_dy = jnp.concatenate(grown_dy, axis=1)
        fading_u = jnp.concatenate(fading_u, axis=1)
        grad_low = grad_inner.astype(bf16)
        gk_ref[rows, 0:STATE] = dot_tn(grad_low, out_keys) + dot_nt(fading_u, later_low)
        gk_ref[rows, STATE : 2 * STATE] = dot_nn(grad_low, in_keys) + dot_nt(grown_dy, start_low)
        ended = jnp.exp(spread_all(end, pairs, low_row))
        st[...] = ended * later + dot_tn(out_keys, grown_dy)
        state_term = jnp.sum(start * later, axis=0, keepdims=True) * ended
        extra = jnp.concatenate(
            [
                state_term + jnp.concatenate(after, axis=1),
                jnp.concatenate(skips, axis=1),
                jnp.zeros((6, width), f32),
            ],
            axis=0,
        )
        extra = dot_nn(extra, sel.astype(f32), highest)
        flows = split_dot(x_buf[0:CHUNK, :], sel)
        direct = split_dot(x_buf[CHUNK : 2 * CHUNK, :], sel)
        grad_log = dot_nn(tri_t, flows, highest) + extra[0:1, :]
        grad_dt = direct + rate * grad_log
        grad_raw = grad_dt * jax.nn.sigmoid(raw_ref[rows, :].astype(f32) + bias)
        graw_ref[rows, :] = grad_raw
        gh_ref[0:1, :] += jnp.sum(grad_raw, axis=0, keepdims=True)
        gh_ref[1:2, :] += jnp.sum(grad_log * dt * rate, axis=0, keepdims=True)
        gh_ref[2:3, :] += extra[1:2, :]
        return skip

    lax.fori_loop(0, chunks, chunk, 0)


def whole_call(body, outs, scratch, cost, *args):
    return pl.pallas_call(
        body,
        out_shape=outs,
        in_specs=[pl.BlockSpec(memory_space=pltpu.VMEM)] * len(args),
        out_specs=jax.tree.map(lambda _: pl.BlockSpec(memory_space=pltpu.VMEM), outs),
        scratch_shapes=scratch,
        cost_estimate=pl.CostEstimate(flops=cost, bytes_accessed=cost // 200, transcendentals=0),
        compiler_params=pltpu.CompilerParams(vmem_limit_bytes=56 * 1024 * 1024),
    )(*args)


def shape(dims, dtype):
    return jax.ShapeDtypeStruct(dims, dtype)


def scan_states(raw, hp, values, keys):
    rows, width = values.shape
    pairs, chunks = width // LANES, rows // CHUNK
    return whole_call(
        functools.partial(states_kernel, pairs, chunks),
        (
            shape((rows, LANES), f32),
            shape((rows, LANES), f32),
            shape((chunks, STATE, width), f32),
            shape((STATE + 16, width), bf16),
        ),
        [pltpu.VMEM((STATE, width), f32)],
        2 * rows * width * STATE,
        raw, hp, values, keys,
    )


def scan_outputs(values, keys, dt, cum, starts, state_in, hp):
    rows, width = values.shape
    pairs, chunks = width // LANES, rows // CHUNK
    return whole_call(
        functools.partial(outputs_kernel, pairs, chunks),
        shape((rows, width), bf16),
        [],
        8 * rows * width * STATE,
        values, keys, dt, cum, starts, state_in, hp,
    )


def scan_direct(grad, keys, cum):
    rows, width = grad.shape
    pairs, chunks = width // LANES, rows // CHUNK
    return whole_call(
        functools.partial(direct_kernel, pairs, chunks),
        shape((STATE + 16, width), bf16),
        [pltpu.VMEM((STATE, width), f32)],
        2 * rows * width * STATE,
        grad, keys, cum,
    )


def scan_back(values, grad, keys, raw, dt, cum, starts, state_in, state_grad, hp):
    rows, width = values.shape
    pairs, chunks = width // LANES, rows // CHUNK
    return whole_call(
        functools.partial(back_kernel, pairs, chunks),
        (
            shape((rows, width), f32),
            shape((rows, 2 * STATE), f32),
            shape((rows, LANES), f32),
            shape((8, LANES), f32),
        ),
        [
            pltpu.VMEM((STATE, width), f32),
            pltpu.VMEM((-(-chunks // 8) * 8, LANES), f32),
            pltpu.VMEM((2 * CHUNK, width), f32),
        ],
        20 * rows * width * STATE,
        values, grad, keys, raw, dt, cum, starts, state_in, state_grad, hp,
    )


def relay_states(packed, by):
    n = lax.axis_size("ctx")
    joined = None
    for k in range(n - 1, 0, -1):
        got = lax.ppermute(packed, "ctx", shift_pairs(n, by * k)).astype(f32)
        state, logs = got[:STATE], jnp.sum(got[STATE:], axis=0, keepdims=True)
        joined = state if joined is None else state + jnp.exp(logs) * joined
    return joined


def rms_scale(values, width):
    return lax.rsqrt(jnp.sum(values * values, axis=-1, keepdims=True) * (1.0 / width) + eps_norm)


def adam_update(weight, grad, moment, square, step_count):
    step_float = step_count[0].astype(f32)
    new_moment = beta_one * moment + (1.0 - beta_one) * grad
    new_square = beta_two * square + (1.0 - beta_two) * grad * grad
    corr_one = 1.0 - jnp.power(jnp.float32(beta_one), step_float)
    corr_two = 1.0 - jnp.power(jnp.float32(beta_two), step_float)
    update = -learn_rate * (
        new_moment / corr_one / (jnp.sqrt(new_square / corr_two) + adam_eps) + decay_rate * weight
    )
    return (grad, new_moment, new_square, update)


def pad_lanes(x, width):
    return jnp.pad(x, ((0, 0), (0, width - x.shape[1])))


def per_device(
    tokens, cotangent, in_weight, out_weight, vectors, in_moment, in_square,
    out_moment, out_square, vec_moment, vec_square, step_count,
):
    seqs = lax.axis_size("seq")
    sidx = lax.axis_index("seq")
    width, heads = INNER // seqs, HEADS // seqs
    padded_width = -(-width // LANES) * LANES
    tok, cot = tokens[0], cotangent[0]
    mine = tok.shape[0]
    block = mine * seqs

    share = vectors.shape[0]
    share_rows = -(-share // (LANES * 16)) * 16
    flat = jnp.pad(vectors, (0, share_rows * LANES - share)).reshape(share_rows, LANES)
    vec = gather_plane_small(flat)
    vec = vec.reshape(-1, share_rows * LANES)[:, :share].reshape(-1).astype(f32)
    tok_all = gather_seq(tok)
    local_in = jnp.concatenate(
        [
            lax.dynamic_slice_in_dim(in_weight, sidx * width, width, 1),
            lax.dynamic_slice_in_dim(in_weight, INNER + sidx * width, width, 1),
            in_weight[:, 2 * INNER : 2 * INNER + 2 * STATE],
            pad_lanes(lax.dynamic_slice_in_dim(in_weight, INNER + CHANNELS + sidx * heads, heads, 1), LANES),
        ],
        axis=1,
    )
    in_cols = gather_plane(local_in)
    out_rows = gather_out_rows(out_weight, width)
    cot_all = gather_seq(cot)

    offset = D
    gain_in = vec[:D]
    conv_weight = vec[offset : offset + CONV * CHANNELS].reshape(CONV, CHANNELS)
    offset += CONV * CHANNELS
    conv_bias = vec[offset : offset + CHANNELS]
    offset += CHANNELS
    gain_out = lax.dynamic_slice_in_dim(vec[offset : offset + INNER], sidx * width, width)
    offset += INNER
    head_rows = vec[offset:].reshape(3, HEADS)
    conv_rows = jnp.concatenate([conv_weight, conv_bias[None]], axis=0)
    conv_rows = jnp.concatenate(
        [lax.dynamic_slice_in_dim(conv_rows, sidx * width, width, 1), conv_rows[:, INNER:]], axis=1
    )
    head_params = jnp.pad(
        lax.dynamic_slice_in_dim(head_rows, sidx * heads, heads, 1), ((0, 5), (0, LANES - heads))
    )

    ahead = lax.ppermute(tok_all[block - 8 :], "ctx", shift_pairs(lax.axis_size("ctx"), 1))
    inputs = jnp.concatenate([ahead, tok_all], axis=0).astype(f32)
    unit_in = inputs * rms_scale(inputs, D)
    normed = (unit_in * gain_in).astype(bf16)
    projected = jnp.dot(normed, in_cols, preferred_element_type=f32).astype(bf16)
    gate = projected[8:, :width]
    mixed_in = projected[8 - (CONV - 1) :, width : 2 * width + 2 * STATE].astype(f32)
    raw = projected[8:, 2 * width + 2 * STATE :]
    conv_sum = conv_rows[CONV] + sum(conv_rows[k] * mixed_in[k : k + block] for k in range(CONV))
    activated = jax.nn.silu(conv_sum).astype(bf16)
    values = pad_lanes(activated[:, :width], padded_width)
    keys = activated[:, width:]

    dt, cum, starts, packed = scan_states(raw, head_params, values, keys)
    state_in = relay_states(packed, 1)
    mixed = scan_outputs(values, keys, dt, cum, starts, state_in, head_params)[:, :width]

    mixed_f, gate_f = mixed.astype(f32), gate.astype(f32)
    sigmoid_gate = jax.nn.sigmoid(gate_f)
    gate_act = gate_f * sigmoid_gate
    gated = mixed_f * gate_act
    grad_normed = lax.dot_general(cot_all, out_rows, (((1,), (1,)), ((), ())), preferred_element_type=f32)
    grad_unit = grad_normed * gain_out
    sums = jnp.stack([jnp.sum(gated * gated, axis=1), jnp.sum(grad_unit * gated, axis=1)])
    sums = exchange(sums, "seq") * (1.0 / INNER)
    scale_out = lax.rsqrt(sums[0] + eps_norm)[:, None]
    unit_out = gated * scale_out
    normed_out = (unit_out * gain_out).astype(bf16)
    gain_out_grad = jnp.sum(grad_normed * unit_out, axis=0)
    grad_gated = scale_out * (grad_unit - unit_out * (sums[1][:, None] * scale_out))
    grad_mixed = (grad_gated * gate_act).astype(bf16)
    grad_gate = (grad_gated * mixed_f * sigmoid_gate * (1.0 + gate_f * (1.0 - sigmoid_gate))).astype(bf16)
    out_part = jnp.dot(normed_out, out_rows, preferred_element_type=f32)
    block_out = (tok.astype(f32) + scatter_seq(out_part)).astype(bf16)

    grad_scan = pad_lanes(grad_mixed, padded_width)
    state_grad = relay_states(scan_direct(grad_scan, keys, cum), -1)
    grad_values, grad_keys, grad_raw, grad_heads = scan_back(
        values, grad_scan, keys, raw, dt, cum, starts, state_in, state_grad, head_params
    )

    grad_act = jnp.concatenate([grad_values[:, :width], grad_keys], axis=1)
    sigmoid_conv = jax.nn.sigmoid(conv_sum)
    grad_conv = grad_act * sigmoid_conv * (1.0 + conv_sum * (1.0 - sigmoid_conv))
    conv_grads = jnp.stack(
        [jnp.sum(grad_conv * mixed_in[k : k + block], axis=0) for k in range(CONV)]
        + [jnp.sum(grad_conv, axis=0)]
    )
    grad_padded = sum(
        jnp.pad(conv_rows[k] * grad_conv, ((k, CONV - 1 - k), (0, 0))) for k in range(CONV)
    )
    rim = lax.ppermute(
        jnp.pad(grad_padded[: CONV - 1], ((0, 8 - (CONV - 1)), (0, 0))).astype(bf16),
        "ctx",
        shift_pairs(lax.axis_size("ctx"), -1),
    )[: CONV - 1].astype(f32)
    grad_mixed_in = (grad_padded[CONV - 1 :] + jnp.pad(rim, ((block - (CONV - 1), 0), (0, 0)))).astype(bf16)
    grad_proj = jnp.concatenate([grad_gate, grad_mixed_in, grad_raw.astype(bf16)], axis=1)

    normed_block = normed[8:]
    in_part = lax.dot_general(normed_block, grad_proj, (((0,), (0,)), ((), ())), preferred_element_type=f32)
    in_owned = scatter_plane(in_part)
    in_all = gather_seq(in_owned.astype(bf16)).astype(f32)
    in_rows = in_weight.shape[0]
    in_all = in_all.reshape(seqs, in_rows, -1)
    in_total = jnp.concatenate(
        [in_all[s, :, :width] for s in range(seqs)]
        + [in_all[s, :, width : 2 * width] for s in range(seqs)]
        + [jnp.sum(in_all[:, :, 2 * width : 2 * width + 2 * STATE], axis=0)]
        + [in_all[s, :, 2 * width + 2 * STATE : 2 * width + 2 * STATE + heads] for s in range(seqs)],
        axis=1,
    )
    out_local = lax.dot_general(normed_out, cot_all, (((0,), (0,)), ((), ())), preferred_element_type=f32)
    planes = lax.axis_size("dp") * lax.axis_size("ctx")
    piece = D // planes
    out_cols = out_local.reshape(width, planes, piece).transpose(1, 0, 2).reshape(planes * width, piece)
    out_owned = gather_seq(scatter_plane(out_cols).astype(bf16))
    out_total = lax.all_to_all(out_owned, PLANE, split_axis=0, concat_axis=1, tiled=True).astype(f32)

    grad_in = lax.dot_general(grad_proj, in_cols, (((1,), (1,)), ((), ())), preferred_element_type=f32)
    gain_in_grad = jnp.sum(grad_in * unit_in[8:], axis=0)
    grad_in = scatter_seq(grad_in) * gain_in
    own = tok.astype(f32)
    scale_own = rms_scale(own, D)
    unit_own = own * scale_own
    token_grad = cot.astype(f32) + scale_own * (
        grad_in - unit_own * jnp.mean(grad_in * unit_own, axis=-1, keepdims=True)
    )

    place_conv = jnp.concatenate(
        [
            lax.dynamic_update_slice_in_dim(
                jnp.zeros((CONV + 1, INNER), f32), conv_grads[:, :width], sidx * width, 1
            ),
            conv_grads[:, width:],
        ],
        axis=1,
    )
    place_gain = lax.dynamic_update_slice_in_dim(jnp.zeros((INNER,), f32), gain_out_grad, sidx * width, 0)
    place_heads = lax.dynamic_update_slice_in_dim(
        jnp.zeros((3, HEADS), f32), grad_heads[:3, :heads], sidx * heads, 1
    )
    vec_local = jnp.concatenate(
        [gain_in_grad, place_conv.reshape(-1), place_gain, place_heads.reshape(-1)]
    )
    length = vec_local.shape[0]
    vec_rows = -(-length // (LANES * 8)) * 8
    vec_sum = jnp.pad(vec_local, (0, vec_rows * LANES - length)).reshape(vec_rows, LANES)
    for axis in ("dp", "ctx", "seq"):
        vec_sum = exchange(vec_sum, axis)
    rank = lax.axis_index("dp") * lax.axis_size("ctx") + lax.axis_index("ctx")
    vec_total = lax.dynamic_slice_in_dim(vec_sum.reshape(-1), rank * share, share)

    in_out = adam_update(in_weight.astype(f32), in_total, in_moment, in_square, step_count)
    out_out = adam_update(out_weight.astype(f32), out_total, out_moment, out_square, step_count)
    vec_out = adam_update(vectors.astype(f32), vec_total, vec_moment, vec_square, step_count)
    return (block_out[None], token_grad[None], *in_out, *out_out, *vec_out)


def solution(mesh):
    rows, weights, vector = P("dp", ("ctx", "seq"), None), P(PLANE, None), P(PLANE)
    in_specs = (
        rows, rows, weights, weights, vector, weights, weights, weights, weights, vector, vector, P(),
    )
    out_specs = (rows, rows) + (weights,) * 8 + (vector,) * 4
    return jax.shard_map(per_device, mesh=mesh, in_specs=in_specs, out_specs=out_specs, check_vma=False)
```

```python
import functools

import jax
import jax.numpy as jnp
from jax import lax
from jax.experimental import pallas as pl
from jax.experimental.pallas import tpu as pltpu
from jax.sharding import PartitionSpec as P

D = 1536
HEADS = 48
HEADDIM = 64
STATE = 128
CONV = 4
CHUNK = 128
LANES = 128
HALO = 16
INNER = HEADS * HEADDIM
CHANNELS = INNER + 2 * STATE
KEYS = 2 * STATE

highest = lax.Precision.HIGHEST
eps_norm = 1e-05
beta_one = 0.9
beta_two = 0.95
adam_eps = 1e-08
decay_rate = 0.1
learn_rate = 0.02
bf16 = jnp.bfloat16
f32 = jnp.float32
PLANE = ("dp", "ctx")
WORLD = ("dp", "ctx", "seq")
CORES = [(0, 1), (1, 0)]
VMEM = pl.BlockSpec(memory_space=pltpu.VMEM)
SMEM = pl.BlockSpec(memory_space=pltpu.SMEM)
ANY = pl.BlockSpec(memory_space=pl.ANY)


def shift_pairs(n, by):
    return [(i, i + by) for i in range(n) if 0 <= i + by < n]


def flip_pairs(n, bit):
    return [(i, i ^ bit) for i in range(n)]


def manual():
    return lax.axis_size("seq") == 4 and lax.axis_size("ctx") == 4 and lax.axis_size("dp") == 2


def ints(*values):
    return jnp.stack([jnp.asarray(v, jnp.int32) for v in values])


def one_piece(x):
    return (x,), ints(0), ints(1)


def line_near(x):
    return (
        lax.ppermute(x, "seq", [(0, 1), (1, 2), (2, 3)]),
        lax.ppermute(x, "seq", [(1, 0), (2, 1), (3, 2)]),
    )


def line_far(near):
    before, after = near
    me = lax.axis_index("seq")
    return (
        lax.ppermute(before, "seq", [(1, 2), (2, 3)]),
        lax.ppermute(after, "seq", [(2, 1), (1, 0)]),
        lax.ppermute(jnp.where(me == 1, before, after), "seq", [(1, 3), (2, 0)]),
    )


def line_pieces(x, near, far):
    me = lax.axis_index("seq")
    across = lax.rem(me + 2, 4)
    places = ints(
        me, jnp.maximum(me - 1, 0), jnp.minimum(me + 1, 3), across, across, jnp.where(me == 0, 3, 0)
    )
    valid = ints(1, me >= 1, me <= 2, me >= 2, me < 2, (me == 0) | (me == 3))
    return (x, *near, *far), places, valid


def line_reduce_far(x):
    me = lax.axis_index("seq")

    def block(b):
        return lax.dynamic_index_in_dim(x, jnp.clip(b, 0, 3), 0, False)

    down = lax.ppermute(block(me - 2), "seq", [(2, 1), (3, 2)])
    up = lax.ppermute(block(me + 2), "seq", [(1, 2), (0, 1)])
    over = lax.ppermute(jnp.where(me == 3, block(0), block(3)), "seq", [(3, 1), (0, 2)])
    return down, up, over


def line_reduce_near(x, far):
    me = lax.axis_index("seq")
    down, up, over = (a.astype(f32) for a in far)

    def block(b):
        return lax.dynamic_index_in_dim(x, jnp.clip(b, 0, 3), 0, False).astype(f32)

    to_left = block(me - 1) + down + jnp.where(me == 1, over, 0.0)
    to_right = block(me + 1) + up + jnp.where(me == 2, over, 0.0)
    return (
        lax.ppermute(to_right.astype(bf16), "seq", [(0, 1), (1, 2), (2, 3)]),
        lax.ppermute(to_left.astype(bf16), "seq", [(1, 0), (2, 1), (3, 2)]),
    )


def line_reduced(x, near):
    mine = lax.dynamic_index_in_dim(x, lax.axis_index("seq"), 0, False).astype(f32)
    return mine + near[0].astype(f32) + near[1].astype(f32)


def plane_pieces(x, others):
    me_d, me_c = lax.axis_index("dp"), lax.axis_index("ctx")
    arrays, places = [x], [me_d * 4 + me_c]
    for (d, c), block in others.items():
        arrays.append(block)
        places.append((me_d ^ d) * 4 + (me_c ^ c))
    return tuple(arrays), ints(*places), ints(*[1] * len(arrays))


def plane_reduce_core(x):
    me_d = lax.axis_index("dp")
    mine = lax.dynamic_slice_in_dim(x, me_d * 4, 4, 0)
    yours = lax.dynamic_slice_in_dim(x, (1 - me_d) * 4, 4, 0)
    got = lax.ppermute(yours, "dp", CORES)
    return (mine.astype(f32) + got.astype(f32)).astype(bf16)


def plane_reduce_send(chip):
    me_c = lax.axis_index("ctx")
    return [
        lax.ppermute(lax.dynamic_index_in_dim(chip, me_c ^ bit, 0, False), "ctx", flip_pairs(4, bit))
        for bit in (3, 1, 2)
    ]


def plane_reduced(chip, got):
    total = lax.dynamic_index_in_dim(chip, lax.axis_index("ctx"), 0, False).astype(f32)
    for part in got:
        total = total + part.astype(f32)
    return total.astype(bf16)


def out_row_pairs():
    first, second, third, fourth = [], [], [], []

    def flat(d, c, s):
        return (d * 4 + c) * 4 + s

    for s in range(4):
        d, y = s // 2, s % 2
        for h in range(2):
            first.append((flat(d, 2 * y + h, s), flat(d, 2 * y + 1 - h, s)))
            second.append((flat(d, 2 * y + h, s), flat(d, 2 * (1 - y) + h, s)))
            third.append((flat(d, 2 * (1 - y) + h, s), flat(d, 2 * (1 - y) + 1 - h, s)))
        for c in range(4):
            fourth.append((flat(d, c, s), flat(1 - d, c, s)))
    return first, second, third, fourth


def owner_pairs(k):
    pairs = []
    for d in range(2):
        for c in range(4):
            g = c ^ k
            for s in range(4):
                pairs.append((((d * 4 + c) * 4 + s), (((g // 2) * 4 + 2 * (g % 2) + d) * 4 + s)))
    return pairs


def total_over(x, axis):
    n = lax.axis_size(axis)
    if not manual():
        return lax.psum(x, axis)
    bit = 1
    while bit < n:
        x = x + lax.ppermute(x, axis, flip_pairs(n, bit))
        bit *= 2
    return x


def sent_states(packed, by):
    n = lax.axis_size("ctx")
    return [lax.ppermute(packed, "ctx", shift_pairs(n, by * k)) for k in range(n - 1, 0, -1)]


def dot_nn(a, b, precision=None):
    return lax.dot_general(
        a, b, (((1,), (0,)), ((), ())), precision=precision, preferred_element_type=f32
    )


def dot_nt(a, b):
    return lax.dot_general(a, b, (((1,), (1,)), ((), ())), preferred_element_type=f32)


def dot_tn(a, b):
    return lax.dot_general(a, b, (((0,), (0,)), ((), ())), preferred_element_type=f32)


def low_lanes(rows):
    return lax.broadcasted_iota(jnp.int32, (rows, LANES), 1) < HEADDIM


def spread(x, pair, low):
    rows = x.shape[0]
    first = jnp.broadcast_to(x[:, 2 * pair : 2 * pair + 1], (rows, LANES))
    second = jnp.broadcast_to(x[:, 2 * pair + 1 : 2 * pair + 2], (rows, LANES))
    return jnp.where(low, first, second)


def spread_all(x, pairs, low):
    return jnp.concatenate([spread(x, j, low) for j in range(pairs)], axis=1)


def softplus(x):
    tail = jnp.exp(-jnp.abs(x))
    one = 1.0 + tail
    rest = one - 1.0
    return jnp.maximum(x, 0.0) + jnp.where(
        rest == 0.0, tail, jnp.log(one) * tail / jnp.where(rest == 0.0, 1.0, rest)
    )


def sigmoid(x):
    return 1.0 / (1.0 + jnp.exp(-x))


def pack_state(pk_ref, state, log_row, pairs, low_row):
    pk_ref[0:STATE, :] = state.astype(bf16)
    total = spread_all(log_row, pairs, low_row)
    high = total.astype(bf16)
    rest = total - high.astype(f32)
    mid = rest.astype(bf16)
    last = (rest - mid.astype(f32)).astype(bf16)
    width = total.shape[1]
    row = lax.broadcasted_iota(jnp.int32, (16, width), 0)
    zero = jnp.zeros((16, width), f32)
    tail = jnp.where(row == 0, high.astype(f32), zero)
    tail = jnp.where(row == 1, mid.astype(f32), tail)
    tail = jnp.where(row == 2, last.astype(f32), tail)
    pk_ref[STATE : STATE + 16, :] = tail.astype(bf16)


def join_states(refs):
    joined = None
    for ref in refs:
        got = ref[...].astype(f32)
        state, logs = got[:STATE], jnp.sum(got[STATE:], axis=0, keepdims=True)
        joined = state if joined is None else state + jnp.exp(logs) * joined
    return joined


def decay_matrix(cum, cum_t, head, causal):
    gap = cum[:, head : head + 1] - cum_t[head : head + 1, :]
    return jnp.where(causal, jnp.exp(jnp.minimum(gap, 0.0)), 0.0)


def stacked(u, low):
    zero = jnp.zeros_like(u)
    return jnp.concatenate([jnp.where(low, u, zero), jnp.where(low, zero, u)], axis=0)


def split_dot(x, sel):
    high = x.astype(bf16)
    rest = (x - high.astype(f32)).astype(bf16)
    return dot_nn(high, sel) + dot_nn(rest, sel)


def chunk_rows(c, lead=0):
    return pl.ds(pl.multiple_of(c * CHUNK + lead, 16), CHUNK)


class Placer:
    def __init__(self, refs, plan_ref, at, rows, buffer, sems):
        self.copies = []
        count = len(refs)
        for i, ref in enumerate(refs):
            place = plan_ref[at + i]
            copy = pltpu.make_async_copy(
                ref, buffer.at[pl.ds(pl.multiple_of(place * rows, 16), ref.shape[0])], sems.at[i]
            )
            self.copies.append((plan_ref[at + count + i], copy))

    def start(self):
        for valid, copy in self.copies:
            pl.when(valid == 1)(copy.start)

    def wait(self):
        for valid, copy in self.copies:
            pl.when(valid == 1)(copy.wait)


def call(body, outs, ins, scratch, flops, *args):
    return pl.pallas_call(
        body,
        out_shape=outs,
        in_specs=ins,
        out_specs=jax.tree.map(lambda _: VMEM, outs),
        scratch_shapes=scratch,
        cost_estimate=pl.CostEstimate(flops=flops, bytes_accessed=flops // 200, transcendentals=0),
        compiler_params=pltpu.CompilerParams(vmem_limit_bytes=58 * 1024 * 1024),
    )(*args)


def shape(dims, dtype):
    return jax.ShapeDtypeStruct(dims, dtype)


def project_kernel(n_tok, n_w, pairs, plan_ref, ahead_ref, gain_ref, conv_ref, hp_ref, *refs):
    tok_refs, w_refs = refs[:n_tok], refs[n_tok : n_tok + n_w]
    normed_ref, proj_ref, v_ref, k_ref, dt_ref, cum_ref, sc_ref, pk_ref = refs[n_tok + n_w : n_tok + n_w + 8]
    x_buf, w_buf, st, tok_sems, w_sems = refs[n_tok + n_w + 8 :]
    width = pairs * LANES
    block = x_buf.shape[0]
    tok = Placer(tok_refs, plan_ref, 0, tok_refs[0].shape[0], x_buf, tok_sems)
    weights = Placer(w_refs, plan_ref, 2 * n_tok, D // 16, w_buf, w_sems)
    tok.start()
    weights.start()
    gain = gain_ref[...]

    def norm(x):
        x = x.astype(f32)
        scale = lax.rsqrt(jnp.sum(x * x, axis=1, keepdims=True) * (1.0 / D) + eps_norm)
        return (x * scale * gain).astype(bf16)

    normed_ref[0:HALO, :] = norm(jnp.concatenate([jnp.zeros((8, D), bf16), ahead_ref[...]], axis=0))
    tok.wait()

    @pl.loop(0, block // CHUNK)
    def _(c):
        normed_ref[chunk_rows(c, HALO), :] = norm(x_buf[chunk_rows(c), :])

    weights.wait()
    cols = w_buf.shape[1]
    step = 512
    rows_all = block + HALO
    row_step = rows_all if rows_all <= 1024 else rows_all // 3
    for r in range(0, rows_all, row_step):
        for n in range(0, cols, 256):
            m = min(256, cols - n)
            proj_ref[r : r + row_step, n : n + m] = dot_nn(
                normed_ref[r : r + row_step, :], w_buf[:, n : n + m]
            ).astype(bf16)

    rate = -jnp.exp(hp_ref[1:2, :])
    bias = hp_ref[0:1, :]
    rows_i = lax.broadcasted_iota(jnp.int32, (CHUNK, CHUNK), 0)
    cols_i = lax.broadcasted_iota(jnp.int32, (CHUNK, CHUNK), 1)
    tri = jnp.where(rows_i >= cols_i, 1.0, 0.0).astype(f32)
    low, low_row = low_lanes(CHUNK), low_lanes(1)
    st[...] = jnp.zeros_like(st)

    def chunk(c, total):
        rows = chunk_rows(c)
        window = pl.ds(pl.multiple_of(c * CHUNK, 16), CHUNK + HALO)
        for n in range(0, width + KEYS, LANES):
            win = proj_ref[window, width + n : width + n + LANES].astype(f32)
            conv = conv_ref[CONV : CONV + 1, n : n + LANES]
            for k in range(CONV):
                conv = conv + conv_ref[k : k + 1, n : n + LANES] * win[HALO - 3 + k : HALO - 3 + k + CHUNK]
            act = (conv * sigmoid(conv)).astype(bf16)
            if n < width:
                v_ref[rows, n : n + LANES] = act
            else:
                k_ref[rows, n - width : n - width + LANES] = act
        raw = proj_ref[chunk_rows(c, HALO), 2 * width + KEYS :].astype(f32)
        dt = softplus(raw + bias)
        cum = dot_nn(tri, dt * rate, highest)
        dt_ref[rows, :] = dt
        cum_ref[rows, :] = cum
        state = st[...]
        sc_ref[c] = state
        end = cum[CHUNK - 1 : CHUNK, :]
        weight = jnp.exp(end - cum) * dt
        scaled = jnp.concatenate(
            [
                (spread(weight, j, low) * v_ref[rows, j * LANES : (j + 1) * LANES].astype(f32)).astype(bf16)
                for j in range(pairs)
            ],
            axis=1,
        )
        fresh = dot_tn(k_ref[rows, 0:STATE], scaled)
        st[...] = jnp.exp(spread_all(end, pairs, low_row)) * state + fresh
        return total + end

    total = lax.fori_loop(0, block // CHUNK, chunk, jnp.zeros((1, LANES), f32))
    pack_state(pk_ref, st[...], total, pairs, low_row)


def project(tok, weights, ahead, gain, conv_rows, hp, width, block):
    pairs, chunks = width // LANES, block // CHUNK
    cols = 2 * width + KEYS + LANES
    plan = jnp.concatenate([tok[1], tok[2], weights[1], weights[2]])
    n_tok, n_w = len(tok[0]), len(weights[0])
    return call(
        functools.partial(project_kernel, n_tok, n_w, pairs),
        (
            shape((HALO + block, D), bf16),
            shape((HALO + block, cols), bf16),
            shape((block, width), bf16),
            shape((block, KEYS), bf16),
            shape((block, LANES), f32),
            shape((block, LANES), f32),
            shape((chunks, STATE, width), f32),
            shape((STATE + 16, width), bf16),
        ),
        [SMEM, VMEM, VMEM, VMEM, VMEM] + [ANY] * (n_tok + n_w),
        [
            pltpu.VMEM((block, D), bf16),
            pltpu.VMEM((D, cols), bf16),
            pltpu.VMEM((STATE, width), f32),
            pltpu.SemaphoreType.DMA((n_tok,)),
            pltpu.SemaphoreType.DMA((n_w,)),
        ],
        2 * block * D * cols,
        plan, ahead, gain, conv_rows, hp, *tok[0], *weights[0],
    )


def inside_kernel(
    n_cot, n_out, pairs, plan_ref, v_ref, k_ref, dt_ref, cum_ref, hp_ref, *refs
):
    cot_refs, out_refs = refs[:n_cot], refs[n_cot : n_cot + n_out]
    y_ref, gn_ref = refs[n_cot + n_out : n_cot + n_out + 2]
    cot_buf, out_buf, cot_sems, out_sems = refs[n_cot + n_out + 2 :]
    block = cot_buf.shape[0]
    cot = Placer(cot_refs, plan_ref, 0, cot_refs[0].shape[0], cot_buf, cot_sems)
    out = Placer(out_refs, plan_ref, 2 * n_cot, out_refs[0].shape[0], out_buf, out_sems)
    cot.start()
    out.start()
    rows_i = lax.broadcasted_iota(jnp.int32, (CHUNK, CHUNK), 0)
    cols_i = lax.broadcasted_iota(jnp.int32, (CHUNK, CHUNK), 1)
    causal = rows_i >= cols_i
    low, low_row = low_lanes(CHUNK), low_lanes(1)

    @pl.loop(0, block // CHUNK)
    def _(c):
        rows = chunk_rows(c)
        dt, cum = dt_ref[rows, :], cum_ref[rows, :]
        cum_t = cum.T
        inner = dot_nt(k_ref[rows, STATE:KEYS], k_ref[rows, 0:STATE])
        for j in range(pairs):
            lanes = slice(j * LANES, (j + 1) * LANES)
            v = v_ref[rows, lanes].astype(f32)
            u = (spread(dt, j, low) * v).astype(bf16)
            weights = jnp.concatenate(
                [(decay_matrix(cum, cum_t, 2 * j + i, causal) * inner).astype(bf16) for i in (0, 1)], axis=1
            )
            y_ref[rows, lanes] = dot_nn(weights, stacked(u, low)) + spread(hp_ref[2:3, :], j, low_row) * v

    cot.wait()
    out.wait()
    tall = min(block, 512)

    @pl.loop(0, block // tall)
    def _(b):
        rows = pl.ds(pl.multiple_of(b * tall, 16), tall)
        for n in range(0, pairs * LANES, 256):
            lanes = slice(n, n + 256)
            gn_ref[rows, lanes] = dot_nt(cot_buf[rows, :], out_buf[lanes, :])


def inside(values, keys, dt, cum, hp, cot, out_rows, block):
    width = values.shape[1]
    pairs = width // LANES
    n_cot, n_out = len(cot[0]), len(out_rows[0])
    plan = jnp.concatenate([cot[1], cot[2], out_rows[1], out_rows[2]])
    return call(
        functools.partial(inside_kernel, n_cot, n_out, pairs),
        (shape((block, width), f32), shape((block, width), f32)),
        [SMEM] + [VMEM] * 5 + [ANY] * (n_cot + n_out),
        [
            pltpu.VMEM((block, D), bf16),
            pltpu.VMEM((width, D), bf16),
            pltpu.SemaphoreType.DMA((n_cot,)),
            pltpu.SemaphoreType.DMA((n_out,)),
        ],
        2 * block * D * width + 8 * block * width * STATE,
        plan, values, keys, dt, cum, hp, *cot[0], *out_rows[0],
    )


def gate_kernel(n_pk, pairs, y_ref, gn_ref, k_ref, cum_ref, sc_ref, proj_ref, gain_ref, *refs):
    pk_refs = refs[:n_pk]
    mixed_ref, sums_ref, sin_ref = refs[n_pk:]
    width = pairs * LANES
    block = y_ref.shape[0]
    sin_ref[...] = join_states(pk_refs)
    low, low_row = low_lanes(CHUNK), low_lanes(1)
    ones = jnp.ones((8, width), bf16)
    row8 = lax.broadcasted_iota(jnp.int32, (8, CHUNK), 0)

    def sum_rows(x):
        high = x.astype(bf16)
        return dot_nt(ones, high) + dot_nt(ones, (x - high.astype(f32)).astype(bf16))

    def chunk(c, offset):
        rows = chunk_rows(c)
        cum = cum_ref[rows, :]
        grown = jnp.exp(cum)
        start = sc_ref[c] + jnp.exp(spread_all(offset, pairs, low_row)) * sin_ref[...]
        carried = dot_nn(k_ref[rows, STATE:KEYS], start.astype(bf16))
        mixed = (y_ref[rows, :] + spread_all(grown, pairs, low) * carried).astype(bf16)
        mixed_ref[rows, :] = mixed
        gate = proj_ref[chunk_rows(c, HALO), 0:width].astype(f32)
        gated = mixed.astype(f32) * (gate * sigmoid(gate))
        first = sum_rows(gated * gated)
        second = sum_rows(gated * (gn_ref[rows, :] * gain_ref[...]))
        sums_ref[:, pl.ds(pl.multiple_of(c * CHUNK, CHUNK), CHUNK)] = jnp.where(
            row8 == 0, first, jnp.where(row8 == 1, second, 0.0)
        )
        return offset + cum[CHUNK - 1 : CHUNK, :]

    lax.fori_loop(0, block // CHUNK, chunk, jnp.zeros((1, LANES), f32))


def gate_forward(y, gn, keys, cum, starts, proj, gain, packed):
    block, width = y.shape
    pairs = width // LANES
    return call(
        functools.partial(gate_kernel, len(packed), pairs),
        (shape((block, width), bf16), shape((8, block), f32), shape((STATE, width), f32)),
        [VMEM] * (7 + len(packed)),
        [],
        8 * block * width * STATE,
        y, gn, keys, cum, starts, proj, gain, *packed,
    )


def norm_kernel(n_sum, pairs, mixed_ref, gn_ref, k_ref, cum_ref, proj_ref, gain_ref, *refs):
    sum_refs = refs[:n_sum]
    no_ref, dy_ref, dg_ref, gg_ref, pk_ref, st = refs[n_sum:]
    width = pairs * LANES
    block = mixed_ref.shape[0]
    chunks = block // CHUNK
    low, low_row = low_lanes(CHUNK), low_lanes(1)
    st[...] = jnp.zeros_like(st)
    gg_ref[...] = jnp.zeros_like(gg_ref)
    gain = gain_ref[...]

    def chunk(i, total):
        c = chunks - 1 - i
        rows = chunk_rows(c)
        lanes = pl.ds(pl.multiple_of(c * CHUNK, CHUNK), CHUNK)
        sums = sum_refs[0][:, lanes]
        for ref in sum_refs[1:]:
            sums = sums + ref[:, lanes]
        sums = jnp.concatenate([sums, jnp.zeros((CHUNK - 8, CHUNK), f32)], axis=0).T * (1.0 / INNER)
        scale = lax.rsqrt(sums[:, 0:1] + eps_norm)
        mean = sums[:, 1:2] * scale
        mixed = mixed_ref[rows, :].astype(f32)
        gate = proj_ref[chunk_rows(c, HALO), 0:width].astype(f32)
        sig = sigmoid(gate)
        act = gate * sig
        unit = mixed * act * scale
        no_ref[rows, :] = (unit * gain).astype(bf16)
        gn = gn_ref[rows, :]
        gg_ref[0:1, :] += jnp.sum(gn * unit, axis=0, keepdims=True)
        grad = scale * (gn * gain - unit * mean)
        dy = (grad * act).astype(bf16)
        dy_ref[rows, :] = dy
        dg_ref[rows, :] = (grad * mixed * sig * (1.0 + gate * (1.0 - sig))).astype(bf16)
        cum = cum_ref[rows, :]
        end = cum[CHUNK - 1 : CHUNK, :]
        scaled = (spread_all(jnp.exp(cum), pairs, low) * dy.astype(f32)).astype(bf16)
        fresh = dot_tn(k_ref[rows, STATE:KEYS], scaled)
        st[...] = jnp.exp(spread_all(end, pairs, low_row)) * st[...] + fresh
        return total + end

    total = lax.fori_loop(0, chunks, chunk, jnp.zeros((1, LANES), f32))
    pack_state(pk_ref, st[...], total, pairs, low_row)


def norm_back(mixed, gn, keys, cum, proj, gain, sums):
    block, width = mixed.shape
    pairs = width // LANES
    return call(
        functools.partial(norm_kernel, len(sums), pairs),
        (
            shape((block, width), bf16),
            shape((block, width), bf16),
            shape((block, width), bf16),
            shape((8, width), f32),
            shape((STATE + 16, width), bf16),
        ),
        [VMEM] * (6 + len(sums)),
        [pltpu.VMEM((STATE, width), f32)],
        4 * block * width * STATE,
        mixed, gn, keys, cum, proj, gain, *sums,
    )


def early_kernel(n_cot, n_out, joined, plan_ref, normed_ref, no_ref, dg_ref, *refs):
    cot_refs, out_refs = refs[:n_cot], refs[n_cot : n_cot + n_out]
    results = refs[n_cot + n_out : -4]
    cot_buf, out_buf, cot_sems, out_sems = refs[-4:]
    cot = Placer(cot_refs, plan_ref, 0, cot_refs[0].shape[0], cot_buf, cot_sems)
    out = Placer(out_refs, plan_ref, 2 * n_cot, out_refs[0].shape[0], out_buf, out_sems)
    out.start()
    cot.start()
    block, width = no_ref.shape
    part_ref = results[0]
    tall = min(block, 512)
    owner = D // 8
    share = width // 8
    gate_rows = normed_ref.shape[0] - HALO
    for g in range(0, D, 384):
        grad = dot_tn(normed_ref[HALO:, g : g + 384], dg_ref[...]).astype(bf16)
        for r in range(0, 384, owner):
            if joined:
                results[1][(g + r) // owner, 0:owner, :] = grad[r : r + owner]
            else:
                results[1][g + r : g + r + owner, :] = grad[r : r + owner]
    out.wait()

    @pl.loop(0, block // tall)
    def _(b):
        rows = pl.ds(pl.multiple_of(b * tall, 16), tall)
        for n in range(0, D, 256):
            part_ref[rows, n : n + 256] = dot_nn(no_ref[rows, :], out_buf[:, n : n + 256]).astype(bf16)

    cot.wait()
    for n in range(0, D, width if joined else 256):
        step = width if joined else 256
        for r in range(0, width, 384 if joined else width):
            tile = 384 if joined else width
            grad = dot_tn(no_ref[:, r : r + tile], cot_buf[:, n : n + step]).astype(bf16)
            if joined:
                half = n // width
                for q in range(0, tile, share):
                    results[1][(r + q) // share, owner + half * share : owner + (half + 1) * share, :] = (
                        grad[q : q + share]
                    )
            else:
                results[2][:, n : n + step] = grad


def early_products(normed, normed_out, grad_gate, cot, out_rows, joined):
    block, width = normed_out.shape
    n_cot, n_out = len(cot[0]), len(out_rows[0])
    plan = jnp.concatenate([cot[1], cot[2], out_rows[1], out_rows[2]])
    if joined:
        grads = (shape((8, 2 * D // 8, width), bf16),)
    else:
        grads = (shape((D, width), bf16), shape((width, D), bf16))
    return call(
        functools.partial(early_kernel, n_cot, n_out, joined),
        (shape((block, D), bf16), *grads),
        [SMEM] + [VMEM] * 3 + [ANY] * (n_cot + n_out),
        [
            pltpu.VMEM((block, D), bf16),
            pltpu.VMEM((width, D), bf16),
            pltpu.SemaphoreType.DMA((n_cot,)),
            pltpu.SemaphoreType.DMA((n_out,)),
        ],
        6 * block * D * width,
        plan, normed, normed_out, grad_gate, *cot[0], *out_rows[0],
    )


def back_kernel(
    n_pk, pairs, v_ref, dy_ref, k_ref, proj_ref, dt_ref, cum_ref, sc_ref, sin_ref, hp_ref, conv_ref, *refs
):
    pk_refs = refs[:n_pk]
    late_ref, rim_ref, cg_ref, gh_ref = refs[n_pk : n_pk + 4]
    st, offs, x_buf, act_buf, gc_buf = refs[n_pk + 4 :]
    width = pairs * LANES
    wide = width + KEYS
    block = v_ref.shape[0]
    chunks = block // CHUNK
    rate = -jnp.exp(hp_ref[1:2, :])
    bias = hp_ref[0:1, :]
    rows_i = lax.broadcasted_iota(jnp.int32, (CHUNK, CHUNK), 0)
    cols_i = lax.broadcasted_iota(jnp.int32, (CHUNK, CHUNK), 1)
    causal, causal_t = rows_i >= cols_i, cols_i >= rows_i
    tri_t = jnp.where(causal_t, 1.0, 0.0).astype(f32)
    low, low_row = low_lanes(CHUNK), low_lanes(1)
    lane_i = lax.broadcasted_iota(jnp.int32, (width, LANES), 0)
    head_i = lax.broadcasted_iota(jnp.int32, (width, LANES), 1)
    owner = (lane_i >= head_i * HEADDIM) & (lane_i < (head_i + 1) * HEADDIM)
    sel = jnp.where(owner, 1.0, 0.0).astype(bf16)
    st[...] = join_states(pk_refs)
    gh_ref[...] = jnp.zeros_like(gh_ref)
    cg_ref[...] = jnp.zeros_like(cg_ref)
    gc_buf[0:8, :] = jnp.zeros((8, wide), f32)
    gc_buf[block + 8 :, :] = jnp.zeros((8, wide), f32)

    def mark(c, offset):
        offs[pl.ds(c, 1), :] = offset
        return offset + cum_ref[pl.ds(c * CHUNK + CHUNK - 1, 1), :]

    lax.fori_loop(0, chunks, mark, jnp.zeros((1, LANES), f32))

    @pl.loop(0, chunks)
    def _(i):
        c = chunks - 1 - i
        rows = chunk_rows(c)
        dt, cum = dt_ref[rows, :], cum_ref[rows, :]
        cum_t = cum.T
        end = cum[CHUNK - 1 : CHUNK, :]
        grown = jnp.exp(cum)
        fading = jnp.exp(end - cum)
        in_keys, out_keys = k_ref[rows, 0:STATE], k_ref[rows, STATE:KEYS]
        inner = dot_nt(out_keys, in_keys)
        inner_t = dot_nt(in_keys, out_keys)
        start = sc_ref[c] + jnp.exp(spread_all(offs[pl.ds(c, 1), :], pairs, low_row)) * sin_ref[...]
        start_low = start.astype(bf16)
        later = st[...]
        later_low = later.astype(bf16)
        carried = dot_nn(out_keys, start_low)
        passed = dot_nn(in_keys, later_low)
        grad_inner = jnp.zeros((CHUNK, CHUNK), f32)
        grown_dy, fading_u, after, skips = [], [], [], []
        for j in range(pairs):
            lanes = slice(j * LANES, (j + 1) * LANES)
            v = v_ref[rows, lanes].astype(f32)
            dy_low = dy_ref[rows, lanes]
            dy = dy_low.astype(f32)
            dt_j, grown_j, fading_j = spread(dt, j, low), spread(grown, j, low), spread(fading, j, low)
            u_low = (dt_j * v).astype(bf16)
            u = u_low.astype(f32)
            u_two = stacked(u_low, low)
            decays, weights, weights_t = [], [], []
            for h in (2 * j, 2 * j + 1):
                gap = cum[:, h : h + 1] - cum_t[h : h + 1, :]
                decay = jnp.where(causal, jnp.exp(jnp.minimum(gap, 0.0)), 0.0)
                decay_t = jnp.where(causal_t, jnp.exp(jnp.minimum(-gap, 0.0)), 0.0)
                decays.append(decay)
                weights.append((decay * inner).astype(bf16))
                weights_t.append((decay_t * inner_t).astype(bf16))
            y = dot_nn(jnp.concatenate(weights, axis=1), u_two) + grown_j * carried[:, lanes]
            du_in = dot_nn(jnp.concatenate(weights_t, axis=1), stacked(dy_low, low))
            du_out = fading_j * passed[:, lanes]
            du = du_in + du_out
            grad_two = dot_nt(dy_low, u_two)
            grad_inner = grad_inner + decays[0] * grad_two[:, :CHUNK] + decays[1] * grad_two[:, CHUNK:]
            x_buf[0:CHUNK, lanes] = dy * y - u * du
            x_buf[CHUNK : 2 * CHUNK, lanes] = v * du
            after.append(jnp.sum(u * du_out, axis=0, keepdims=True))
            skips.append(jnp.sum(dy * v, axis=0, keepdims=True))
            grown_dy.append((grown_j * dy).astype(bf16))
            fading_u.append((fading_j * u).astype(bf16))
            act_buf[:, lanes] = dt_j * du + spread(hp_ref[2:3, :], j, low_row) * dy
        grown_dy = jnp.concatenate(grown_dy, axis=1)
        fading_u = jnp.concatenate(fading_u, axis=1)
        grad_low = grad_inner.astype(bf16)
        act_buf[:, width : width + STATE] = dot_tn(grad_low, out_keys) + dot_nt(fading_u, later_low)
        act_buf[:, width + STATE :] = dot_nn(grad_low, in_keys) + dot_nt(grown_dy, start_low)
        ended = jnp.exp(spread_all(end, pairs, low_row))
        st[...] = ended * later + dot_tn(out_keys, grown_dy)
        state_term = jnp.sum(start * later, axis=0, keepdims=True) * ended
        extra = jnp.concatenate(
            [
                state_term + jnp.concatenate(after, axis=1),
                jnp.concatenate(skips, axis=1),
                jnp.zeros((6, width), f32),
            ],
            axis=0,
        )
        extra = split_dot(extra, sel)
        flows = split_dot(x_buf[0:CHUNK, :], sel)
        direct = split_dot(x_buf[CHUNK : 2 * CHUNK, :], sel)
        grad_log = dot_nn(tri_t, flows, highest) + extra[0:1, :]
        grad_dt = direct + rate * grad_log
        grad_raw = grad_dt * sigmoid(proj_ref[chunk_rows(c, HALO), width + wide :].astype(f32) + bias)
        late_ref[rows, wide:] = grad_raw.astype(bf16)
        gh_ref[0:1, :] += jnp.sum(grad_raw, axis=0, keepdims=True)
        gh_ref[1:2, :] += jnp.sum(grad_log * dt * rate, axis=0, keepdims=True)
        gh_ref[2:3, :] += extra[1:2, :]

        window = pl.ds(pl.multiple_of(c * CHUNK, 16), CHUNK + HALO)
        for n in range(0, wide, LANES):
            lanes = slice(n, n + LANES)
            win = proj_ref[window, width + n : width + n + LANES].astype(f32)
            taps = [conv_ref[k : k + 1, lanes] for k in range(CONV)]
            moved = [win[HALO - 3 + k : HALO - 3 + k + CHUNK] for k in range(CONV)]
            conv = conv_ref[CONV : CONV + 1, lanes] + sum(t * m for t, m in zip(taps, moved))
            sig = sigmoid(conv)
            gc = act_buf[:, lanes] * (sig * (1.0 + conv * (1.0 - sig)))
            gc_buf[pl.ds(pl.multiple_of(c * CHUNK + 8, 8), CHUNK), lanes] = gc
            for k in range(CONV):
                cg_ref[k : k + 1, lanes] += jnp.sum(gc * moved[k], axis=0, keepdims=True)
            cg_ref[CONV : CONV + 1, lanes] += jnp.sum(gc, axis=0, keepdims=True)
            span = gc_buf[pl.ds(pl.multiple_of(c * CHUNK + 8, 8), CHUNK + 8), lanes]
            late_ref[rows, lanes] = sum(
                taps[k] * span[CONV - 1 - k : CONV - 1 - k + CHUNK] for k in range(CONV)
            ).astype(bf16)

    row8 = lax.broadcasted_iota(jnp.int32, (8, LANES), 0)
    for n in range(0, wide, LANES):
        lanes = slice(n, n + LANES)
        span = gc_buf[0:24, lanes]
        rim = sum(conv_ref[k : k + 1, lanes] * span[8 - k : 16 - k] for k in range(CONV))
        rim_ref[:, lanes] = jnp.where(row8 < CONV - 1, rim, 0.0).astype(bf16)


def scan_back(values, dy, keys, proj, dt, cum, starts, state_in, hp, conv_rows, packed):
    block, width = values.shape
    pairs, chunks = width // LANES, block // CHUNK
    wide = width + KEYS
    return call(
        functools.partial(back_kernel, len(packed), pairs),
        (
            shape((block, wide + LANES), bf16),
            shape((8, wide), bf16),
            shape((8, wide), f32),
            shape((8, LANES), f32),
        ),
        [VMEM] * (10 + len(packed)),
        [
            pltpu.VMEM((STATE, width), f32),
            pltpu.VMEM((-(-chunks // 8) * 8, LANES), f32),
            pltpu.VMEM((2 * CHUNK, width), f32),
            pltpu.VMEM((CHUNK, wide), f32),
            pltpu.VMEM((block + 16, wide), f32),
        ],
        40 * block * width * STATE,
        values, dy, keys, proj, dt, cum, starts, state_in, hp, conv_rows, *packed,
    )


def with_rim(late_ref, rim_ref, buffer):
    block = late_ref.shape[0]
    wide = rim_ref.shape[1]
    buffer[...] = late_ref[...]
    rim = jnp.concatenate([rim_ref[...].astype(f32), jnp.zeros((8, wide), f32)], axis=0)
    rim = pltpu.roll(rim, HALO - (CONV - 1), 0)
    last = late_ref[block - HALO :, 0:wide].astype(f32) + rim
    buffer[block - HALO :, 0:wide] = last.astype(bf16)


def late_kernel(normed_ref, late_ref, rim_ref, out_ref, buffer):
    with_rim(late_ref, rim_ref, buffer)
    cols = late_ref.shape[1]
    owner = D // 8
    for g in range(0, D, 384):
        for n in range(0, cols, 384):
            m = min(384, cols - n)
            grad = dot_tn(normed_ref[HALO:, g : g + 384], buffer[:, n : n + m]).astype(bf16)
            for r in range(0, 384, owner):
                out_ref[(g + r) // owner, :, n : n + m] = grad[r : r + owner]


def late_products(normed, late, rim):
    block, cols = late.shape
    return call(
        late_kernel,
        shape((8, D // 8, cols), bf16),
        [VMEM] * 3,
        [pltpu.VMEM((block, cols), bf16)],
        2 * block * D * cols,
        normed, late, rim,
    )


def input_kernel(n_w, plan_ref, normed_ref, dg_ref, late_ref, rim_ref, gain_ref, *refs):
    w_refs = refs[:n_w]
    gi_ref, gg_ref, buffer, w_buf, sems = refs[n_w:]
    weights = Placer(w_refs, plan_ref, 0, D // 16, w_buf, sems)
    weights.start()
    with_rim(late_ref, rim_ref, buffer)
    block, width = dg_ref.shape
    gg_ref[...] = jnp.zeros_like(gg_ref)
    weights.wait()
    tall = min(block, 512)
    for b in range(0, block, tall):
        for n in range(0, D, 256):
            lanes = slice(n, n + 256)
            grad = dot_nt(dg_ref[b : b + tall, :], w_buf[lanes, :width])
            grad = grad + dot_nt(buffer[b : b + tall, :], w_buf[lanes, width:])
            unit = normed_ref[HALO + b : HALO + b + tall, lanes].astype(f32) / gain_ref[:, lanes]
            gg_ref[0:1, lanes] += jnp.sum(grad * unit, axis=0, keepdims=True)
            gi_ref[b : b + tall, lanes] = grad.astype(bf16)


def input_products(normed, grad_gate, late, rim, gain, weights):
    block, cols = late.shape
    width = grad_gate.shape[1]
    n_w = len(weights[0])
    plan = jnp.concatenate([weights[1], weights[2]])
    return call(
        functools.partial(input_kernel, n_w),
        (shape((block, D), bf16), shape((8, D), f32)),
        [SMEM] + [VMEM] * 5 + [ANY] * n_w,
        [
            pltpu.VMEM((block, cols), bf16),
            pltpu.VMEM((D, width + cols), bf16),
            pltpu.SemaphoreType.DMA((n_w,)),
        ],
        2 * block * D * (cols + width),
        plan, normed, grad_gate, late, rim, gain, *weights[0],
    )


def adam_rates(step_count):
    step_float = step_count[0].astype(f32)
    corr_one = 1.0 - jnp.power(jnp.float32(beta_one), step_float)
    corr_two = 1.0 - jnp.power(jnp.float32(beta_two), step_float)
    return jnp.stack([1.0 / corr_one, 1.0 / corr_two])


def adam_math(weight, grad, moment, square, one, two):
    new_moment = beta_one * moment + (1.0 - beta_one) * grad
    new_square = beta_two * square + (1.0 - beta_two) * grad * grad
    update = -learn_rate * (
        new_moment * one / (jnp.sqrt(new_square * two) + adam_eps) + decay_rate * weight
    )
    return grad, new_moment, new_square, update


def adam_plain(weight, grad, moment, square, rates):
    return adam_math(weight.astype(f32), grad, moment, square, rates[0], rates[1])


def adam_in_kernel(n, width, heads, plan_ref, rate_ref, w_ref, m_ref, s_ref, *refs):
    early, late = refs[:n], refs[n : 2 * n]
    outs = refs[2 * n : 2 * n + 4]
    g, = refs[2 * n + 4 :]
    rows = w_ref.shape[0]
    keys_at, steps_at = 2 * INNER, 2 * INNER + KEYS
    g[:, keys_at:] = jnp.zeros((rows, g.shape[1] - keys_at), f32)
    lane = lax.broadcasted_iota(jnp.int32, (rows, LANES), 1)
    for i in range(n):

        @pl.when(plan_ref[n + i] == 1)
        def _():
            place = plan_ref[i]
            at = pl.multiple_of(place * width, LANES)
            g[:, pl.ds(at, width)] = early[i][...].astype(f32)
            g[:, pl.ds(INNER + at, width)] = late[i][:, 0:width].astype(f32)
            g[:, keys_at:steps_at] += late[i][:, width : width + KEYS].astype(f32)
            steps = jnp.where(lane < heads, late[i][:, width + KEYS :].astype(f32), 0.0)
            g[:, steps_at:] += pltpu.roll(steps, place * heads, 1)

    one, two = rate_ref[0], rate_ref[1]
    cols = w_ref.shape[1]
    for c in range(0, cols, 512):
        lanes = slice(c, min(c + 512, cols))
        results = adam_math(
            w_ref[:, lanes].astype(f32), g[:, lanes], m_ref[:, lanes], s_ref[:, lanes], one, two
        )
        for ref, value in zip(outs, results):
            ref[:, lanes] = value


def adam_in(weight, moment, square, rates, early, late, width, heads):
    rows, cols = weight.shape
    tile = 32
    n = len(early[0])
    plan = jnp.concatenate([early[1], early[2]])
    whole = pl.BlockSpec((tile, cols), lambda i: (i, 0))
    return pl.pallas_call(
        functools.partial(adam_in_kernel, n, width, heads),
        grid=(rows // tile,),
        out_shape=[shape((rows, cols), f32)] * 4,
        in_specs=[SMEM, SMEM, whole, whole, whole]
        + [pl.BlockSpec((tile, a.shape[1]), lambda i: (i, 0)) for a in (*early[0], *late[0])],
        out_specs=[whole] * 4,
        scratch_shapes=[pltpu.VMEM((tile, 2 * INNER + KEYS + LANES), f32)],
        cost_estimate=pl.CostEstimate(flops=rows * cols * 20, bytes_accessed=rows * cols * 28, transcendentals=0),
        compiler_params=pltpu.CompilerParams(vmem_limit_bytes=58 * 1024 * 1024),
    )(plan, rates, weight, moment, square, *early[0], *late[0])


def adam_out_kernel(pos_ref, rate_ref, w_ref, m_ref, s_ref, *refs):
    pieces, outs = refs[:4], refs[4:8]
    g, = refs[8:]
    rows, cols = w_ref.shape
    width = pieces[0].shape[1]
    for k in range(4):

        @pl.when((pos_ref[0] ^ pl.program_id(0)) == k)
        def _():
            for half in range(cols // width):
                g[:, half * width : (half + 1) * width] = pieces[k][half * rows : (half + 1) * rows, :].astype(f32)

    one, two = rate_ref[0], rate_ref[1]
    for c in range(0, cols, 512):
        lanes = slice(c, min(c + 512, cols))
        results = adam_math(
            w_ref[:, lanes].astype(f32), g[:, lanes], m_ref[:, lanes], s_ref[:, lanes], one, two
        )
        for ref, value in zip(outs, results):
            ref[:, lanes] = value


def adam_out(weight, moment, square, rates, group, pieces):
    rows, cols = weight.shape
    tile = rows // 4
    whole = pl.BlockSpec((tile, cols), lambda i: (i, 0))
    return pl.pallas_call(
        adam_out_kernel,
        grid=(4,),
        out_shape=[shape((rows, cols), f32)] * 4,
        in_specs=[SMEM, SMEM, whole, whole, whole] + [pl.BlockSpec(p.shape, lambda i: (0, 0)) for p in pieces],
        out_specs=[whole] * 4,
        scratch_shapes=[pltpu.VMEM((tile, cols), f32)],
        cost_estimate=pl.CostEstimate(flops=rows * cols * 20, bytes_accessed=rows * cols * 28, transcendentals=0),
        compiler_params=pltpu.CompilerParams(vmem_limit_bytes=58 * 1024 * 1024),
    )(group, rates, weight, moment, square, *pieces)


def pad_lanes(x, width):
    return x if x.shape[1] == width else jnp.pad(x, ((0, 0), (0, width - x.shape[1])))


def after(values, *earlier):
    return lax.optimization_barrier((values, earlier))[0]


def gather_all(tok, cot, local_in, out_weight, flat, width):
    me, me_c, me_d = lax.axis_index("seq"), lax.axis_index("ctx"), lax.axis_index("dp")
    vec_parts = [flat] + [lax.ppermute(flat, "ctx", flip_pairs(4, bit)) for bit in (1, 2, 3)]
    tok_near = line_near(tok)
    w_x = lax.ppermute(local_in, "ctx", flip_pairs(4, 1))
    w_y = lax.ppermute(local_in, "ctx", flip_pairs(4, 2))
    w_d = lax.ppermute(local_in, "dp", CORES)
    cot_near = line_near(cot)
    tok_near, w_x, w_y, vec_parts, out_weight = lax.optimization_barrier(
        (tok_near, w_x, w_y, vec_parts, out_weight)
    )
    vec_own = jnp.concatenate(vec_parts, axis=0)
    vec_other = lax.ppermute(vec_own, "dp", CORES)
    tok_far = line_far(tok_near)
    half = local_in.shape[0] // 2
    w_up = lax.ppermute(w_y[:half], "ctx", flip_pairs(4, 1))
    w_down = lax.ppermute(w_x[half:], "ctx", flip_pairs(4, 2))
    w_xd, w_yd = lax.ppermute(w_x, "dp", CORES), lax.ppermute(w_y, "dp", CORES)
    first, second, third, fourth = out_row_pairs()
    beside = lax.ppermute(out_weight, WORLD, first)
    along = lax.ppermute(out_weight, WORLD, second)
    tok_far, w_up, w_down, cot_near = lax.optimization_barrier((tok_far, w_up, w_down, cot_near))
    w_upd, w_downd = lax.ppermute(w_up, "dp", CORES), lax.ppermute(w_down, "dp", CORES)
    tail = tok.shape[0] - 8
    last = jnp.where(
        me == 3,
        tok[tail:],
        jnp.where(me == 2, tok_near[1][tail:], jnp.where(me == 1, tok_far[1][tail:], tok_far[2][tail:])),
    )
    ahead = lax.ppermute(last, "ctx", shift_pairs(4, 1))
    cot_far = line_far(cot_near)
    beyond = lax.ppermute(along, WORLD, third)
    source = (me_d == me // 2) & (me_c // 2 == lax.rem(me, 2))
    near_core = me_d == me // 2
    mine = jnp.where(source, out_weight, along)
    other = jnp.where(source, beside, beyond)
    mine_back = lax.ppermute(mine, WORLD, fourth)
    other_back = lax.ppermute(other, WORLD, fourth)
    x = lax.rem(me_c, 2)
    out_rows = (
        (mine, other, mine_back, other_back),
        ints(x, 1 - x, x, 1 - x),
        ints(near_core, near_core, 1 - near_core, 1 - near_core),
    )
    places = []
    for d, c, part in (
        (0, 0, 0), (0, 1, 0), (0, 2, 0), (0, 3, 0), (0, 3, 1),
        (1, 0, 0), (1, 1, 0), (1, 2, 0), (1, 3, 0), (1, 3, 1),
    ):
        places.append(((me_d ^ d) * 4 + (me_c ^ c)) * 2 + part)
    arrays = (local_in, w_x, w_y, w_up, w_down, w_d, w_xd, w_yd, w_upd, w_downd)
    in_cols = (arrays, ints(*places), ints(*[1] * len(arrays)))
    share_rows = flat.shape[0]
    vec = jnp.zeros((8, share_rows, LANES), flat.dtype)
    for d, rows in ((0, vec_own), (1, vec_other)):
        for c in range(4):
            block = rows[c * share_rows : (c + 1) * share_rows][None]
            vec = lax.dynamic_update_slice_in_dim(vec, block, (me_d ^ d) * 4 + (me_c ^ c), 0)
    return line_pieces(tok, tok_near, tok_far), line_pieces(cot, cot_near, cot_far), in_cols, out_rows, ahead, vec


def gather_all_plain(tok, cot, local_in, out_weight, flat, width):
    sidx = lax.axis_index("seq")
    tok_all = lax.all_gather(tok, "seq", axis=0, tiled=True)
    cot_all = lax.all_gather(cot, "seq", axis=0, tiled=True)
    in_cols = lax.all_gather(local_in, PLANE, axis=0, tiled=True)
    real = INNER // lax.axis_size("seq")
    out_rows = lax.dynamic_slice_in_dim(
        lax.all_gather(out_weight, PLANE, axis=0, tiled=True), sidx * real, real, 0
    )
    out_rows = jnp.pad(out_rows, ((0, width - real), (0, 0)))
    ahead = lax.ppermute(tok_all[-8:], "ctx", shift_pairs(lax.axis_size("ctx"), 1))
    vec = lax.all_gather(flat, PLANE, axis=0, tiled=True).reshape(-1, *flat.shape)
    return one_piece(tok_all), one_piece(cot_all), one_piece(in_cols), one_piece(out_rows), ahead, vec


def per_device(
    tokens, cotangent, in_weight, out_weight, vectors, in_moment, in_square,
    out_moment, out_square, vec_moment, vec_square, step_count,
):
    seqs, sidx = lax.axis_size("seq"), lax.axis_index("seq")
    real, heads = INNER // seqs, HEADS // seqs
    width = -(-real // LANES) * LANES
    tok, cot = tokens[0], cotangent[0]
    block = tok.shape[0] * seqs
    by_hand = manual()

    share = vectors.shape[0]
    share_rows = -(-share // (LANES * 16)) * 16
    flat = jnp.pad(vectors, (0, share_rows * LANES - share)).reshape(share_rows, LANES)
    local_in = jnp.concatenate(
        [
            pad_lanes(lax.dynamic_slice_in_dim(in_weight, sidx * real, real, 1), width),
            pad_lanes(lax.dynamic_slice_in_dim(in_weight, INNER + sidx * real, real, 1), width),
            in_weight[:, 2 * INNER : 2 * INNER + KEYS],
            pad_lanes(lax.dynamic_slice_in_dim(in_weight, INNER + CHANNELS + sidx * heads, heads, 1), LANES),
        ],
        axis=1,
    )
    gather = gather_all if by_hand else gather_all_plain
    tok_parts, cot_parts, in_cols, out_rows, ahead, vec = gather(tok, cot, local_in, out_weight, flat, width)

    vec = vec.reshape(-1, share_rows * LANES)[:, :share].reshape(-1).astype(f32)
    offset = D
    gain_in = vec[:D][None]
    conv_weight = vec[offset : offset + (CONV + 1) * CHANNELS].reshape(CONV + 1, CHANNELS)
    offset += (CONV + 1) * CHANNELS
    gain_out = pad_lanes(lax.dynamic_slice_in_dim(vec[offset : offset + INNER], sidx * real, real)[None], width)
    offset += INNER
    head_rows = vec[offset:].reshape(3, HEADS)
    conv_rows = jnp.concatenate(
        [
            pad_lanes(lax.dynamic_slice_in_dim(conv_weight, sidx * real, real, 1), width),
            conv_weight[:, INNER:],
        ],
        axis=1,
    )
    conv_rows = jnp.pad(conv_rows, ((0, 3), (0, 0)))
    head_params = jnp.pad(
        lax.dynamic_slice_in_dim(head_rows, sidx * heads, heads, 1), ((0, 5), (0, LANES - heads))
    )

    normed, proj, values, keys, dt, cum, starts, packed = project(
        tok_parts, in_cols, ahead, gain_in, conv_rows, head_params, width, block
    )
    sent = sent_states(packed, 1)
    y_inside, grad_normed = inside(values, keys, dt, cum, head_params, cot_parts, out_rows, block)
    mixed, sums, state_in = gate_forward(y_inside, grad_normed, keys, cum, starts, proj, gain_out, sent)
    if by_hand:
        all_sums = [sums] + [lax.ppermute(sums, "seq", flip_pairs(4, bit)) for bit in (3, 2, 1)]
    else:
        all_sums = [lax.psum(sums, "seq")]

    normed_out, grad_mixed, grad_gate, gain_out_grad, packed = norm_back(
        mixed, grad_normed, keys, cum, proj, gain_out, all_sums
    )
    sent = sent_states(packed, -1)
    early = early_products(normed, normed_out, grad_gate, cot_parts, out_rows, by_hand)
    part = early[0].reshape(seqs, -1, D)
    if by_hand:
        part_far = line_reduce_far(part)
        early_chip = plane_reduce_core(early[1])
        early_got = plane_reduce_send(early_chip)

    late, rim, conv_grads, grad_heads = scan_back(
        values, grad_mixed, keys, proj, dt, cum, starts, state_in, head_params, conv_rows, sent
    )
    rim = lax.ppermute(rim, "ctx", shift_pairs(lax.axis_size("ctx"), -1))
    if by_hand:
        part_near = line_reduce_near(part, part_far)
        early_mine = plane_reduced(early_chip, early_got)
        early_near = line_near(early_mine)

    in_late = late_products(normed, late, rim)
    grad_in, gain_in_grad = input_products(normed, grad_gate, late, rim, gain_in, in_cols)
    grad_in = grad_in.reshape(seqs, -1, D)
    rates = adam_rates(step_count)
    in_rows = in_weight.shape[0]
    rank = lax.axis_index("dp") * lax.axis_size("ctx") + lax.axis_index("ctx")
    if by_hand:
        late_chip = plane_reduce_core(in_late)
        block_sum = line_reduced(part, part_near)
        late_got = plane_reduce_send(late_chip)
        in_far = line_reduce_far(grad_in)
        early_far = line_far(early_near)
        early_pieces = line_pieces(early_mine, early_near, early_far)
        ordered = jnp.zeros((4, in_rows, width), bf16)
        me = sidx
        slots = [
            (me, early_mine),
            (lax.rem(me + 3, 4), jnp.where(me == 0, early_far[2], early_near[0])),
            (lax.rem(me + 1, 4), jnp.where(me == 3, early_far[2], early_near[1])),
            (lax.rem(me + 2, 4), jnp.where(me < 2, early_far[1], early_far[0])),
        ]
        for place, piece in slots:
            ordered = lax.dynamic_update_slice_in_dim(ordered, piece[in_rows:][None], place, 0)
        me_c = lax.axis_index("ctx")
        out_pieces = [
            lax.ppermute(lax.dynamic_index_in_dim(ordered, me_c ^ k, 0, False), WORLD, owner_pairs(k))
            for k in range(4)
        ]
        in_near = line_reduce_near(grad_in, in_far)
        late_mine = plane_reduced(late_chip, late_got)
        late_near = line_near(late_mine)
        input_sum = line_reduced(grad_in, in_near)
        late_far = line_far(late_near)
        late_pieces = line_pieces(late_mine, late_near, late_far)
        in_out = adam_in(in_weight, in_moment, in_square, rates, early_pieces, late_pieces, width, heads)
        out_out = adam_out(out_weight, out_moment, out_square, rates, ints(rank // 2), out_pieces)
    else:
        block_sum = lax.psum_scatter(part, "seq", scatter_dimension=0).astype(f32)
        input_sum = lax.psum_scatter(grad_in, "seq", scatter_dimension=0).astype(f32)
        grads = jnp.concatenate([early[1].reshape(8, in_rows, width), in_late], axis=2)
        grads = lax.psum_scatter(grads, PLANE, scatter_dimension=0)
        grads = lax.all_gather(grads, "seq").astype(f32)
        steps_at = 2 * width + KEYS
        in_total = jnp.concatenate(
            [grads[s, :, :real] for s in range(seqs)]
            + [grads[s, :, width : width + real] for s in range(seqs)]
            + [jnp.sum(grads[:, :, 2 * width : steps_at], axis=0)]
            + [grads[s, :, steps_at : steps_at + heads] for s in range(seqs)],
            axis=1,
        )
        out_cols = early[2][:real].reshape(real, 8, D // 8).transpose(1, 0, 2)
        out_cols = lax.psum_scatter(out_cols, PLANE, scatter_dimension=0)
        out_cols = lax.all_gather(out_cols, "seq", axis=0, tiled=True)
        out_total = lax.all_to_all(out_cols, PLANE, split_axis=0, concat_axis=1, tiled=True).astype(f32)
        in_out = adam_plain(in_weight, in_total, in_moment, in_square, rates)
        out_out = adam_plain(out_weight, out_total, out_moment, out_square, rates)

    block_out = (tok.astype(f32) + block_sum).astype(bf16)
    grad_unit = input_sum * gain_in
    own = tok.astype(f32)
    scale = lax.rsqrt(jnp.mean(own * own, axis=1, keepdims=True) + eps_norm)
    unit = own * scale
    token_grad = cot.astype(f32) + scale * (grad_unit - unit * jnp.mean(grad_unit * unit, axis=1, keepdims=True))

    conv_place = jnp.concatenate(
        [
            lax.dynamic_update_slice_in_dim(
                jnp.zeros((CONV + 1, INNER), f32), conv_grads[: CONV + 1, :real], sidx * real, 1
            ),
            conv_grads[: CONV + 1, width:],
        ],
        axis=1,
    )
    gain_place = lax.dynamic_update_slice_in_dim(
        jnp.zeros((INNER,), f32), gain_out_grad[0, :real], sidx * real, 0
    )
    head_place = lax.dynamic_update_slice_in_dim(
        jnp.zeros((3, HEADS), f32), grad_heads[:3, :heads], sidx * heads, 1
    )
    vec_local = jnp.concatenate([gain_in_grad[0], conv_place.reshape(-1), gain_place, head_place.reshape(-1)])
    length = vec_local.shape[0]
    vec_rows = -(-length // (LANES * 8)) * 8
    vec_sum = jnp.pad(vec_local, (0, vec_rows * LANES - length)).reshape(vec_rows, LANES)
    for axis in ("dp", "ctx", "seq"):
        vec_sum = total_over(vec_sum, axis)
    vec_total = lax.dynamic_slice_in_dim(vec_sum.reshape(-1), rank * share, share)
    vec_out = adam_plain(vectors, vec_total, vec_moment, vec_square, rates)
    return (block_out[None], token_grad[None], *in_out, *out_out, *vec_out)


def solution(mesh):
    rows, weights, vector = P("dp", ("ctx", "seq"), None), P(PLANE, None), P(PLANE)
    in_specs = (
        rows, rows, weights, weights, vector, weights, weights, weights, weights, vector, vector, P(),
    )
    out_specs = (rows, rows) + (weights,) * 8 + (vector,) * 4
    return jax.shard_map(per_device, mesh=mesh, in_specs=in_specs, out_specs=out_specs, check_vma=False)
```

```python
import functools
import math

import jax
import jax.numpy as jnp
import numpy as np
from jax import lax
from jax.experimental import pallas as pl
from jax.experimental.pallas import tpu as pltpu
from jax.sharding import PartitionSpec as P


D = 1536
HEADS = 48
HEADDIM = 64
STATE = 128
CONV = 4
CHUNK = 128
LANES = 128
HALO = 16
VEC_ROWS = 168
INNER = HEADS * HEADDIM
CHANNELS = INNER + 2 * STATE
KEYS = 2 * STATE

highest = lax.Precision.HIGHEST
eps_norm = 1e-05
beta_one = 0.9
beta_two = 0.95
adam_eps = 1e-08
decay_rate = 0.1
learn_rate = 0.02
bf16 = jnp.bfloat16
f32 = jnp.float32
PLANE = ("dp", "ctx")
WORLD = ("dp", "ctx", "seq")
CORES = [(0, 1), (1, 0)]
VMEM = pl.BlockSpec(memory_space=pltpu.VMEM)
SMEM = pl.BlockSpec(memory_space=pltpu.SMEM)
ANY = pl.BlockSpec(memory_space=pl.ANY)


def shift_pairs(n, by):
    return [(i, i + by) for i in range(n) if 0 <= i + by < n]


def flip_pairs(n, bit):
    return [(i, i ^ bit) for i in range(n)]


def manual():
    return lax.axis_size("seq") == 4 and lax.axis_size("ctx") == 4 and lax.axis_size("dp") == 2


LINE_AT, COLS_AT, ROWS_AT, CORE_AT, SEQ_AT, PLAN = 0, 12, 32, 40, 41, 64
COL_PARTS = (
    (0, 0, 0), (0, 1, 0), (0, 2, 0), (0, 3, 0), (0, 3, 1),
    (1, 0, 0), (1, 1, 0), (1, 2, 0), (1, 3, 0), (1, 3, 1),
)


def plan_row(me_d, me_c, me):
    across = (me + 2) % 4
    row = [me, max(me - 1, 0), min(me + 1, 3), across, across, 3 if me == 0 else 0]
    row += [1, me >= 1, me <= 2, me >= 2, me < 2, me in (0, 3)]
    row += [((me_d ^ d) * 4 + (me_c ^ c)) * 2 + part for d, c, part in COL_PARTS]
    row += [1] * len(COL_PARTS)
    x, near = me_c % 2, me_d == me // 2
    row += [x, 1 - x, x, 1 - x, near, near, not near, not near, me_d, me]
    return [int(v) for v in row] + [0] * (PLAN - len(row))


def device_plan():
    if not manual():
        core = lax.axis_index("dp").astype(jnp.int32)
        return jnp.zeros((PLAN,), jnp.int32).at[1].set(1).at[CORE_AT].set(core)
    table = np.array([[[plan_row(d, c, s) for s in range(4)] for c in range(4)] for d in range(2)], np.int32)
    rank = (lax.axis_index("dp") * 4 + lax.axis_index("ctx")) * 4 + lax.axis_index("seq")
    return lax.dynamic_index_in_dim(jnp.asarray(table.reshape(32, PLAN)), rank, 0, False)


def line_near(x):
    return (lax.ppermute(x, "seq", [(0, 1), (1, 2), (2, 3)]), lax.ppermute(x, "seq", [(1, 0), (2, 1), (3, 2)]))


def line_far(near):
    before, after = near
    me = lax.axis_index("seq")
    return (
        lax.ppermute(before, "seq", [(1, 2), (2, 3)]),
        lax.ppermute(after, "seq", [(2, 1), (1, 0)]),
        lax.ppermute(jnp.where(me == 1, before, after), "seq", [(1, 3), (2, 0)]),
    )


def line_pieces(x, near, far):
    return (x, *near, *far), LINE_AT


def line_reduce_far(x):
    me = lax.axis_index("seq")

    def block(b):
        return lax.dynamic_index_in_dim(x, jnp.clip(b, 0, 3), 0, False)

    down = lax.ppermute(block(me - 2), "seq", [(2, 1), (3, 2)])
    up = lax.ppermute(block(me + 2), "seq", [(1, 2), (0, 1)])
    over = lax.ppermute(block(jnp.where(me == 3, 0, 3)), "seq", [(3, 1), (0, 2)])
    return down, up, over


def line_reduce_near(x, far):
    me = lax.axis_index("seq")
    down, up, over = (a.astype(f32) for a in far)

    def block(b):
        return lax.dynamic_index_in_dim(x, jnp.clip(b, 0, 3), 0, False).astype(f32)

    to_left = block(me - 1) + down + jnp.where(me == 1, over, 0.0)
    to_right = block(me + 1) + up + jnp.where(me == 2, over, 0.0)
    return (
        lax.ppermute(to_right.astype(bf16), "seq", [(0, 1), (1, 2), (2, 3)]),
        lax.ppermute(to_left.astype(bf16), "seq", [(1, 0), (2, 1), (3, 2)]),
    )


def line_reduce_direct(x):
    me = lax.axis_index("seq")
    return [
        lax.ppermute(lax.dynamic_index_in_dim(x, me ^ bit, 0, False), "seq", flip_pairs(4, bit))
        for bit in (3, 2, 1)
    ]


def hold(values, until):
    return lax.optimization_barrier((values, until))[0]


def line_reduced(x, near):
    mine = lax.dynamic_index_in_dim(x, lax.axis_index("seq"), 0, False).astype(f32)
    for part in near:
        mine = mine + part.astype(f32)
    return mine


def plane_reduce_core(mine, yours):
    got = lax.ppermute(yours, "dp", CORES)
    return (mine.astype(f32) + got.astype(f32)).astype(bf16)


def plane_reduce_send(chip):
    me_c = lax.axis_index("ctx")
    return [
        lax.ppermute(lax.dynamic_index_in_dim(chip, me_c ^ bit, 0, False), "ctx", flip_pairs(4, bit))
        for bit in (3, 1, 2)
    ]


def plane_reduced(chip, got):
    total = lax.dynamic_index_in_dim(chip, lax.axis_index("ctx"), 0, False).astype(f32)
    for part in got:
        total = total + part.astype(f32)
    return total.astype(bf16)


def out_row_pairs():
    first, second, third, fourth = [], [], [], []

    def flat(d, c, s):
        return (d * 4 + c) * 4 + s

    for s in range(4):
        d, y = s // 2, s % 2
        for h in range(2):
            first.append((flat(d, 2 * y + h, s), flat(d, 2 * y + 1 - h, s)))
            second.append((flat(d, 2 * y + h, s), flat(d, 2 * (1 - y) + h, s)))
            third.append((flat(d, 2 * (1 - y) + h, s), flat(d, 2 * (1 - y) + 1 - h, s)))
        for c in range(4):
            fourth.append((flat(d, c, s), flat(1 - d, c, s)))
    return first, second, third, fourth


def owner_pairs(k):
    pairs = []
    for d in range(2):
        for c in range(4):
            g = c ^ k
            for s in range(4):
                pairs.append((((d * 4 + c) * 4 + s), (((g // 2) * 4 + 2 * (g % 2) + d) * 4 + s)))
    return pairs


def total_over(x, axis, until=None):
    n = lax.axis_size(axis)
    if not manual():
        return lax.psum(x, axis)
    got = [lax.ppermute(x, axis, flip_pairs(n, bit)) for bit in range(n - 1, 0, -1)]
    if until is not None:
        got = hold(got, until)
    return x + functools.reduce(jnp.add, got)


def sent_states(packed, by):
    n = lax.axis_size("ctx")
    return [lax.ppermute(packed, "ctx", shift_pairs(n, by * k)) for k in range(n - 1, 0, -1)]


def dot_nn(a, b, precision=None):
    return lax.dot_general(
        a, b, (((1,), (0,)), ((), ())), precision=precision, preferred_element_type=f32
    )


def dot_nt(a, b):
    return lax.dot_general(a, b, (((1,), (1,)), ((), ())), preferred_element_type=f32)


def dot_tn(a, b):
    return lax.dot_general(a, b, (((0,), (0,)), ((), ())), preferred_element_type=f32)


def low_lanes(rows):
    return lax.broadcasted_iota(jnp.int32, (rows, LANES), 1) < HEADDIM


def spread(x, pair, low):
    rows = x.shape[0]
    first = jnp.broadcast_to(x[:, 2 * pair : 2 * pair + 1], (rows, LANES))
    second = jnp.broadcast_to(x[:, 2 * pair + 1 : 2 * pair + 2], (rows, LANES))
    return jnp.where(low, first, second)


def spread_all(x, pairs, low):
    return jnp.concatenate([spread(x, j, low) for j in range(pairs)], axis=1)


def softplus(x):
    tail = jnp.exp(-jnp.abs(x))
    one = 1.0 + tail
    rest = one - 1.0
    return jnp.maximum(x, 0.0) + jnp.where(
        rest == 0.0, tail, jnp.log(one) * tail / jnp.where(rest == 0.0, 1.0, rest)
    )


def sigmoid(x):
    return 1.0 / (1.0 + jnp.exp(-x))


def pack_state(pk_ref, state, log_row, pairs, low_row):
    pk_ref[0:STATE, :] = state.astype(bf16)
    total = spread_all(log_row, pairs, low_row)
    high = total.astype(bf16)
    rest = total - high.astype(f32)
    mid = rest.astype(bf16)
    last = (rest - mid.astype(f32)).astype(bf16)
    width = total.shape[1]
    row = lax.broadcasted_iota(jnp.int32, (16, width), 0)
    zero = jnp.zeros((16, width), f32)
    tail = jnp.where(row == 0, high.astype(f32), zero)
    tail = jnp.where(row == 1, mid.astype(f32), tail)
    tail = jnp.where(row == 2, last.astype(f32), tail)
    pk_ref[STATE : STATE + 16, :] = tail.astype(bf16)


def join_states(refs):
    joined = None
    for ref in refs:
        got = ref[...].astype(f32)
        state, logs = got[:STATE], jnp.sum(got[STATE:], axis=0, keepdims=True)
        joined = state if joined is None else state + jnp.exp(logs) * joined
    return joined


def decay_matrix(cum, cum_t, head, causal):
    gap = cum[:, head : head + 1] - cum_t[head : head + 1, :]
    return jnp.where(causal, jnp.exp(jnp.minimum(gap, 0.0)), 0.0)


def stacked(u, low):
    zero = jnp.zeros_like(u)
    return jnp.concatenate([jnp.where(low, u, zero), jnp.where(low, zero, u)], axis=0)


def split_dot(x, sel):
    high = x.astype(bf16)
    rest = (x - high.astype(f32)).astype(bf16)
    return dot_nn(high, sel) + dot_nn(rest, sel)


def chunk_rows(c, lead=0):
    return pl.ds(pl.multiple_of(c * CHUNK + lead, 16), CHUNK)


class Placer:
    def __init__(self, refs, plan_ref, at, rows, buffer, sems):
        self.copies = []
        count = len(refs)
        for i, ref in enumerate(refs):
            place = plan_ref[at + i]
            copy = pltpu.make_async_copy(
                ref, buffer.at[pl.ds(pl.multiple_of(place * rows, 16), ref.shape[0])], sems.at[i]
            )
            self.copies.append((plan_ref[at + count + i], copy))

    def start(self):
        for valid, copy in self.copies:
            pl.when(valid == 1)(copy.start)

    def wait(self):
        for valid, copy in self.copies:
            pl.when(valid == 1)(copy.wait)


def held_bytes(*arrays):
    return sum(math.prod(a.shape) * jnp.dtype(a.dtype).itemsize for a in arrays)


def call(body, outs, ins, scratch, flops, *args):
    held = held_bytes(*jax.tree.leaves(outs), *(a for a, spec in zip(args, ins) if spec is VMEM))
    held += held_bytes(*(a for a in scratch if not isinstance(a, pltpu.SemaphoreType)
                         and jnp.issubdtype(a.dtype, jnp.floating)))
    limit = min(58, MARGIN + held * 9 // 8 // 1024**2) * 1024**2
    return pl.pallas_call(
        body,
        out_shape=outs,
        in_specs=ins,
        out_specs=jax.tree.map(lambda _: VMEM, outs),
        scratch_shapes=scratch,
        cost_estimate=pl.CostEstimate(flops=flops, bytes_accessed=flops // 200, transcendentals=0),
        compiler_params=pltpu.CompilerParams(vmem_limit_bytes=limit),
    )(*args)


MARGIN = 10


def shape(dims, dtype):
    return jax.ShapeDtypeStruct(dims, dtype)


def project_kernel(n_tok, n_w, tok_at, w_at, plan_ref, gain_ref, *refs):
    tok_refs, w_refs = refs[:n_tok], refs[n_tok : n_tok + n_w]
    normed_ref, gate_ref, mixed_ref, raw_ref = refs[n_tok + n_w : n_tok + n_w + 4]
    x_buf, w_buf, tok_sems, w_sems = refs[n_tok + n_w + 4 :]
    block = x_buf.shape[0]
    tok = Placer(tok_refs, plan_ref, tok_at, tok_refs[0].shape[0], x_buf, tok_sems)
    weights = Placer(w_refs, plan_ref, w_at, D // 16, w_buf, w_sems)
    tok.start()
    weights.start()
    gain = gain_ref[...]

    def norm(x):
        x = x.astype(f32)
        scale = lax.rsqrt(jnp.sum(x * x, axis=1, keepdims=True) * (1.0 / D) + eps_norm)
        return (x * scale * gain).astype(bf16)

    tok.wait()

    @pl.loop(0, block // CHUNK)
    def _(c):
        normed_ref[chunk_rows(c), :] = norm(x_buf[chunk_rows(c), :])

    weights.wait()
    row_step = min(block, 512)
    at = 0
    for ref in (gate_ref, mixed_ref, raw_ref):
        for r in range(0, block, row_step):
            for n in range(0, ref.shape[1], 256):
                m = min(256, ref.shape[1] - n)
                ref[r : r + row_step, n : n + m] = dot_nn(
                    normed_ref[r : r + row_step, :], w_buf[:, at + n : at + n + m]
                ).astype(bf16)
        at += ref.shape[1]


def project(plan, tok, weights, gain, width, block):
    cols = 2 * width + KEYS + LANES
    n_tok, n_w = len(tok[0]), len(weights[0])
    return call(
        functools.partial(project_kernel, n_tok, n_w, tok[1], weights[1]),
        tuple(shape((block, n), bf16) for n in (D, width, width + KEYS, LANES)),
        [SMEM, VMEM] + [ANY] * (n_tok + n_w),
        [
            pltpu.VMEM((block, D), bf16),
            pltpu.VMEM((D, cols), bf16),
            pltpu.SemaphoreType.DMA((n_tok,)),
            pltpu.SemaphoreType.DMA((n_w,)),
        ],
        2 * block * D * cols,
        plan, gain, *tok[0], *weights[0],
    )


def conv_kernel(
    pairs, mixed_in_ref, ahead_ref, raw_ref, conv_ref, hp_ref, v_ref, k_ref, dt_ref, cum_ref, sc_ref, pk_ref, st, mixed_ref
):
    width = pairs * LANES
    block = v_ref.shape[0]
    mixed_ref[0:HALO, :] = ahead_ref[...]
    mixed_ref[HALO:, :] = mixed_in_ref[...]
    rate = -jnp.exp(hp_ref[1:2, :])
    bias = hp_ref[0:1, :]
    rows_i = lax.broadcasted_iota(jnp.int32, (CHUNK, CHUNK), 0)
    cols_i = lax.broadcasted_iota(jnp.int32, (CHUNK, CHUNK), 1)
    tri = jnp.where(rows_i >= cols_i, 1.0, 0.0).astype(f32)
    low, low_row = low_lanes(CHUNK), low_lanes(1)
    st[...] = jnp.zeros_like(st)

    def chunk(c, total):
        rows = chunk_rows(c)
        window = pl.ds(pl.multiple_of(c * CHUNK, 16), CHUNK + HALO)
        for n in range(0, width + KEYS, LANES):
            win = mixed_ref[window, n : n + LANES].astype(f32)
            conv = conv_ref[CONV : CONV + 1, n : n + LANES]
            for k in range(CONV):
                conv = conv + conv_ref[k : k + 1, n : n + LANES] * win[HALO - 3 + k : HALO - 3 + k + CHUNK]
            act = (conv * sigmoid(conv)).astype(bf16)
            if n < width:
                v_ref[rows, n : n + LANES] = act
            else:
                k_ref[rows, n - width : n - width + LANES] = act
        raw = raw_ref[chunk_rows(c), :].astype(f32)
        dt = softplus(raw + bias)
        cum = dot_nn(tri, dt * rate, highest)
        dt_ref[rows, :] = dt
        cum_ref[rows, :] = cum
        state = st[...]
        sc_ref[c] = state
        end = cum[CHUNK - 1 : CHUNK, :]
        weight = jnp.exp(end - cum) * dt
        scaled = jnp.concatenate(
            [
                (spread(weight, j, low) * v_ref[rows, j * LANES : (j + 1) * LANES].astype(f32)).astype(bf16)
                for j in range(pairs)
            ],
            axis=1,
        )
        fresh = dot_tn(k_ref[rows, 0:STATE], scaled)
        st[...] = jnp.exp(spread_all(end, pairs, low_row)) * state + fresh
        return total + end

    total = lax.fori_loop(0, block // CHUNK, chunk, jnp.zeros((1, LANES), f32))
    pack_state(pk_ref, st[...], total, pairs, low_row)


def convolve(mixed_in, ahead, raw, conv_rows, hp, width, block):
    pairs, chunks = width // LANES, block // CHUNK
    return call(
        functools.partial(conv_kernel, pairs),
        (
            shape((block, width), bf16),
            shape((block, KEYS), bf16),
            shape((block, LANES), f32),
            shape((block, LANES), f32),
            shape((chunks, STATE, width), f32),
            shape((STATE + 16, width), bf16),
        ),
        [VMEM] * 5,
        [pltpu.VMEM((STATE, width), f32), pltpu.VMEM((HALO + block, width + KEYS), bf16)],
        12 * block * width * STATE,
        mixed_in, ahead, raw, conv_rows, hp,
    )


def inside_kernel(pairs, v_ref, k_ref, dt_ref, cum_ref, hp_ref, y_ref):
    rows_i = lax.broadcasted_iota(jnp.int32, (CHUNK, CHUNK), 0)
    cols_i = lax.broadcasted_iota(jnp.int32, (CHUNK, CHUNK), 1)
    causal = rows_i >= cols_i
    low, low_row = low_lanes(CHUNK), low_lanes(1)

    @pl.loop(0, v_ref.shape[0] // CHUNK)
    def _(c):
        rows = chunk_rows(c)
        dt, cum = dt_ref[rows, :], cum_ref[rows, :]
        cum_t = cum.T
        inner = dot_nt(k_ref[rows, STATE:KEYS], k_ref[rows, 0:STATE])
        for j in range(pairs):
            lanes = slice(j * LANES, (j + 1) * LANES)
            v = v_ref[rows, lanes].astype(f32)
            u = (spread(dt, j, low) * v).astype(bf16)
            weights = jnp.concatenate(
                [(decay_matrix(cum, cum_t, 2 * j + i, causal) * inner).astype(bf16) for i in (0, 1)], axis=1
            )
            y_ref[rows, lanes] = dot_nn(weights, stacked(u, low)) + spread(hp_ref[2:3, :], j, low_row) * v


def inside(values, keys, dt, cum, hp):
    block, width = values.shape
    return call(
        functools.partial(inside_kernel, width // LANES),
        shape((block, width), f32),
        [VMEM] * 5,
        [],
        8 * block * width * STATE,
        values, keys, dt, cum, hp,
    )


def cot_kernel(n_cot, n_out, cot_at, out_at, plan_ref, *refs):
    cot_refs, out_refs = refs[:n_cot], refs[n_cot : n_cot + n_out]
    gn_ref, cot_buf, out_buf, cot_sems, out_sems = refs[n_cot + n_out :]
    block = cot_buf.shape[0]
    cot = Placer(cot_refs, plan_ref, cot_at, cot_refs[0].shape[0], cot_buf, cot_sems)
    out = Placer(out_refs, plan_ref, out_at, out_refs[0].shape[0], out_buf, out_sems)
    cot.start()
    out.start()
    cot.wait()
    out.wait()
    tall = min(block, 512)

    @pl.loop(0, block // tall)
    def _(b):
        rows = pl.ds(pl.multiple_of(b * tall, 16), tall)
        for n in range(0, gn_ref.shape[1], 256):
            lanes = slice(n, n + 256)
            gn_ref[rows, lanes] = dot_nt(cot_buf[rows, :], out_buf[lanes, :])


def cot_product(plan, cot, out_rows, width, block):
    n_cot, n_out = len(cot[0]), len(out_rows[0])
    return call(
        functools.partial(cot_kernel, n_cot, n_out, cot[1], out_rows[1]),
        shape((block, width), f32),
        [SMEM] + [ANY] * (n_cot + n_out),
        [
            pltpu.VMEM((block, D), bf16),
            pltpu.VMEM((width, D), bf16),
            pltpu.SemaphoreType.DMA((n_cot,)),
            pltpu.SemaphoreType.DMA((n_out,)),
        ],
        2 * block * D * width,
        plan, *cot[0], *out_rows[0],
    )


def gate_kernel(n_pk, pairs, y_ref, gn_ref, k_ref, cum_ref, sc_ref, gate_ref, gain_ref, *refs):
    pk_refs = refs[:n_pk]
    mixed_ref, sums_ref, sin_ref = refs[n_pk:]
    block = y_ref.shape[0]
    sin_ref[...] = join_states(pk_refs)
    low, low_row = low_lanes(CHUNK), low_lanes(1)
    lane = lax.broadcasted_iota(jnp.int32, (CHUNK, LANES), 1)

    def chunk(c, offset):
        rows = chunk_rows(c)
        cum = cum_ref[rows, :]
        grown = jnp.exp(cum)
        start = sc_ref[c] + jnp.exp(spread_all(offset, pairs, low_row)) * sin_ref[...]
        carried = dot_nn(k_ref[rows, STATE:KEYS], start.astype(bf16))
        mixed = (y_ref[rows, :] + spread_all(grown, pairs, low) * carried).astype(bf16)
        mixed_ref[rows, :] = mixed
        gate = gate_ref[chunk_rows(c), :].astype(f32)
        gated = mixed.astype(f32) * (gate * sigmoid(gate))
        first = jnp.sum(gated * gated, axis=1, keepdims=True)
        second = jnp.sum(gated * (gn_ref[rows, :] * gain_ref[...]), axis=1, keepdims=True)
        both = jnp.where(lane == 0, first, jnp.where(lane == 1, second, 0.0)).T
        sums_ref[:, pl.ds(pl.multiple_of(c * CHUNK, CHUNK), CHUNK)] = both[0:8]
        return offset + cum[CHUNK - 1 : CHUNK, :]

    lax.fori_loop(0, block // CHUNK, chunk, jnp.zeros((1, LANES), f32))


def gate_forward(y, gn, keys, cum, starts, gate, gain, packed):
    block, width = y.shape
    pairs = width // LANES
    return call(
        functools.partial(gate_kernel, len(packed), pairs),
        (shape((block, width), bf16), shape((8, block), f32), shape((STATE, width), f32)),
        [VMEM] * (7 + len(packed)),
        [],
        8 * block * width * STATE,
        y, gn, keys, cum, starts, gate, gain, *packed,
    )


def norm_kernel(n_sum, pairs, mixed_ref, gn_ref, k_ref, cum_ref, gate_ref, gain_ref, *refs):
    sum_refs = refs[:n_sum]
    no_ref, dy_ref, dg_ref, gg_ref, pk_ref, st = refs[n_sum:]
    block = mixed_ref.shape[0]
    chunks = block // CHUNK
    low, low_row = low_lanes(CHUNK), low_lanes(1)
    st[...] = jnp.zeros_like(st)
    gg_ref[...] = jnp.zeros_like(gg_ref)
    gain = gain_ref[...]

    def chunk(i, total):
        c = chunks - 1 - i
        rows = chunk_rows(c)
        lanes = pl.ds(pl.multiple_of(c * CHUNK, CHUNK), CHUNK)
        sums = sum_refs[0][:, lanes]
        for ref in sum_refs[1:]:
            sums = sums + ref[:, lanes]
        sums = jnp.concatenate([sums, jnp.zeros((CHUNK - 8, CHUNK), f32)], axis=0).T * (1.0 / INNER)
        scale = lax.rsqrt(sums[:, 0:1] + eps_norm)
        mean = sums[:, 1:2] * scale
        mixed = mixed_ref[rows, :].astype(f32)
        gate = gate_ref[chunk_rows(c), :].astype(f32)
        sig = sigmoid(gate)
        act = gate * sig
        unit = mixed * act * scale
        no_ref[rows, :] = (unit * gain).astype(bf16)
        gn = gn_ref[rows, :]
        gg_ref[0:1, :] += jnp.sum(gn * unit, axis=0, keepdims=True)
        grad = scale * (gn * gain - unit * mean)
        dy = (grad * act).astype(bf16)
        dy_ref[rows, :] = dy
        dg_ref[rows, :] = (grad * mixed * sig * (1.0 + gate * (1.0 - sig))).astype(bf16)
        cum = cum_ref[rows, :]
        end = cum[CHUNK - 1 : CHUNK, :]
        scaled = (spread_all(jnp.exp(cum), pairs, low) * dy.astype(f32)).astype(bf16)
        fresh = dot_tn(k_ref[rows, STATE:KEYS], scaled)
        st[...] = jnp.exp(spread_all(end, pairs, low_row)) * st[...] + fresh
        return total + end

    total = lax.fori_loop(0, chunks, chunk, jnp.zeros((1, LANES), f32))
    pack_state(pk_ref, st[...], total, pairs, low_row)


def norm_back(mixed, gn, keys, cum, gate, gain, sums):
    block, width = mixed.shape
    pairs = width // LANES
    return call(
        functools.partial(norm_kernel, len(sums), pairs),
        (
            shape((block, width), bf16),
            shape((block, width), bf16),
            shape((block, width), bf16),
            shape((8, width), f32),
            shape((STATE + 16, width), bf16),
        ),
        [VMEM] * (6 + len(sums)),
        [pltpu.VMEM((STATE, width), f32)],
        4 * block * width * STATE,
        mixed, gn, keys, cum, gate, gain, *sums,
    )


def early_kernel(n_cot, cot_at, joined, plan_ref, normed_ref, no_ref, dg_ref, *refs):
    cot_refs = refs[:n_cot]
    results = refs[n_cot:-2]
    cot_buf, cot_sems = refs[-2:]
    cot = Placer(cot_refs, plan_ref, cot_at, cot_refs[0].shape[0], cot_buf, cot_sems)
    cot.start()
    width = no_ref.shape[1]
    if not joined:
        for g in range(0, D, 384):
            results[0][g : g + 384, :] = dot_tn(normed_ref[:, g : g + 384], dg_ref[...]).astype(bf16)
        cot.wait()
        for n in range(0, D, 256):
            results[1][:, n : n + 256] = dot_tn(no_ref[...], cot_buf[:, n : n + 256]).astype(bf16)
        return
    core = plan_ref[CORE_AT]
    owner, share = D // 8, width // 8
    for side, ref in enumerate(results):
        base = (core ^ side) * (D // 2)
        for g in range(0, D // 2, 2 * owner):
            at = pl.ds(pl.multiple_of(base + g, LANES), 2 * owner)
            grad = dot_tn(normed_ref[:, at], dg_ref[...]).astype(bf16)
            for r in range(0, 2 * owner, owner):
                ref[(g + r) // owner, 0:owner, :] = grad[r : r + owner]
    cot.wait()
    for side, ref in enumerate(results):
        at = pl.ds(pl.multiple_of((core ^ side) * (width // 2), LANES), width // 2)
        for n in range(0, D, width):
            grad = dot_tn(no_ref[:, at], cot_buf[:, n : n + width]).astype(bf16)
            half = owner + n // width * share
            for q in range(0, width // 2, share):
                ref[q // share, half : half + share, :] = grad[q : q + share]


def early_products(plan, normed, normed_out, grad_gate, cot, joined):
    block, width = normed_out.shape
    n_cot = len(cot[0])
    if joined:
        grads = (shape((4, 2 * D // 8, width), bf16),) * 2
    else:
        grads = (shape((D, width), bf16), shape((width, D), bf16))
    return call(
        functools.partial(early_kernel, n_cot, cot[1], joined),
        grads,
        [SMEM] + [VMEM] * 3 + [ANY] * n_cot,
        [pltpu.VMEM((block, D), bf16), pltpu.SemaphoreType.DMA((n_cot,))],
        4 * block * D * width,
        plan, normed, normed_out, grad_gate, *cot[0],
    )


def part_kernel(n_out, out_at, plan_ref, no_ref, *refs):
    out_refs = refs[:n_out]
    part_ref, out_buf, out_sems = refs[n_out:]
    out = Placer(out_refs, plan_ref, out_at, out_refs[0].shape[0], out_buf, out_sems)
    out.start()
    out.wait()
    block = no_ref.shape[0]
    tall = min(block, 512)

    @pl.loop(0, block // tall)
    def _(b):
        rows = pl.ds(pl.multiple_of(b * tall, 16), tall)
        for n in range(0, D, 256):
            part_ref[rows, n : n + 256] = dot_nn(no_ref[rows, :], out_buf[:, n : n + 256]).astype(bf16)


def out_product(plan, normed_out, out_rows):
    block, width = normed_out.shape
    n_out = len(out_rows[0])
    return call(
        functools.partial(part_kernel, n_out, out_rows[1]),
        shape((block, D), bf16),
        [SMEM, VMEM] + [ANY] * n_out,
        [pltpu.VMEM((width, D), bf16), pltpu.SemaphoreType.DMA((n_out,))],
        2 * block * D * width,
        plan, normed_out, *out_rows[0],
    )


def back_kernel(
    n_pk, pairs, v_ref, dy_ref, k_ref, step_ref, dt_ref, cum_ref, sc_ref, sin_ref, hp_ref, *refs
):
    pk_refs = refs[:n_pk]
    act_ref, raw_ref, gh_ref = refs[n_pk : n_pk + 3]
    st, offs, x_buf = refs[n_pk + 3 :]
    width = pairs * LANES
    block = v_ref.shape[0]
    chunks = block // CHUNK
    rate = -jnp.exp(hp_ref[1:2, :])
    bias = hp_ref[0:1, :]
    rows_i = lax.broadcasted_iota(jnp.int32, (CHUNK, CHUNK), 0)
    cols_i = lax.broadcasted_iota(jnp.int32, (CHUNK, CHUNK), 1)
    causal, causal_t = rows_i >= cols_i, cols_i >= rows_i
    tri_t = jnp.where(causal_t, 1.0, 0.0).astype(f32)
    low, low_row = low_lanes(CHUNK), low_lanes(1)
    lane_i = lax.broadcasted_iota(jnp.int32, (width, LANES), 0)
    head_i = lax.broadcasted_iota(jnp.int32, (width, LANES), 1)
    owner = (lane_i >= head_i * HEADDIM) & (lane_i < (head_i + 1) * HEADDIM)
    sel = jnp.where(owner, 1.0, 0.0).astype(bf16)
    st[...] = join_states(pk_refs)
    gh_ref[...] = jnp.zeros_like(gh_ref)

    def mark(c, offset):
        offs[pl.ds(c, 1), :] = offset
        return offset + cum_ref[pl.ds(c * CHUNK + CHUNK - 1, 1), :]

    lax.fori_loop(0, chunks, mark, jnp.zeros((1, LANES), f32))

    @pl.loop(0, chunks)
    def _(i):
        c = chunks - 1 - i
        rows = chunk_rows(c)
        dt, cum = dt_ref[rows, :], cum_ref[rows, :]
        cum_t = cum.T
        end = cum[CHUNK - 1 : CHUNK, :]
        grown = jnp.exp(cum)
        fading = jnp.exp(end - cum)
        in_keys, out_keys = k_ref[rows, 0:STATE], k_ref[rows, STATE:KEYS]
        inner = dot_nt(out_keys, in_keys)
        inner_t = dot_nt(in_keys, out_keys)
        start = sc_ref[c] + jnp.exp(spread_all(offs[pl.ds(c, 1), :], pairs, low_row)) * sin_ref[...]
        start_low = start.astype(bf16)
        later = st[...]
        later_low = later.astype(bf16)
        carried = dot_nn(out_keys, start_low)
        passed = dot_nn(in_keys, later_low)
        grad_inner = jnp.zeros((CHUNK, CHUNK), f32)
        grown_dy, fading_u, after, skips = [], [], [], []
        for j in range(pairs):
            lanes = slice(j * LANES, (j + 1) * LANES)
            v = v_ref[rows, lanes].astype(f32)
            dy_low = dy_ref[rows, lanes]
            dy = dy_low.astype(f32)
            dt_j, grown_j, fading_j = spread(dt, j, low), spread(grown, j, low), spread(fading, j, low)
            u_low = (dt_j * v).astype(bf16)
            u = u_low.astype(f32)
            u_two = stacked(u_low, low)
            decays, weights, weights_t = [], [], []
            for h in (2 * j, 2 * j + 1):
                gap = cum[:, h : h + 1] - cum_t[h : h + 1, :]
                decay = jnp.where(causal, jnp.exp(jnp.minimum(gap, 0.0)), 0.0)
                decay_t = jnp.where(causal_t, jnp.exp(jnp.minimum(-gap, 0.0)), 0.0)
                decays.append(decay)
                weights.append((decay * inner).astype(bf16))
                weights_t.append((decay_t * inner_t).astype(bf16))
            y = dot_nn(jnp.concatenate(weights, axis=1), u_two) + grown_j * carried[:, lanes]
            du_in = dot_nn(jnp.concatenate(weights_t, axis=1), stacked(dy_low, low))
            du_out = fading_j * passed[:, lanes]
            du = du_in + du_out
            grad_two = dot_nt(dy_low, u_two)
            grad_inner = grad_inner + decays[0] * grad_two[:, :CHUNK] + decays[1] * grad_two[:, CHUNK:]
            x_buf[0:CHUNK, lanes] = dy * y - u * du
            x_buf[CHUNK : 2 * CHUNK, lanes] = v * du
            after.append(jnp.sum(u * du_out, axis=0, keepdims=True))
            skips.append(jnp.sum(dy * v, axis=0, keepdims=True))
            grown_dy.append((grown_j * dy).astype(bf16))
            fading_u.append((fading_j * u).astype(bf16))
            act_ref[rows, lanes] = dt_j * du + spread(hp_ref[2:3, :], j, low_row) * dy
        grown_dy = jnp.concatenate(grown_dy, axis=1)
        fading_u = jnp.concatenate(fading_u, axis=1)
        grad_low = grad_inner.astype(bf16)
        act_ref[rows, width : width + STATE] = dot_tn(grad_low, out_keys) + dot_nt(fading_u, later_low)
        act_ref[rows, width + STATE :] = dot_nn(grad_low, in_keys) + dot_nt(grown_dy, start_low)
        ended = jnp.exp(spread_all(end, pairs, low_row))
        st[...] = ended * later + dot_tn(out_keys, grown_dy)
        state_term = jnp.sum(start * later, axis=0, keepdims=True) * ended
        extra = jnp.concatenate(
            [
                state_term + jnp.concatenate(after, axis=1),
                jnp.concatenate(skips, axis=1),
                jnp.zeros((6, width), f32),
            ],
            axis=0,
        )
        extra = split_dot(extra, sel)
        flows = split_dot(x_buf[0:CHUNK, :], sel)
        direct = split_dot(x_buf[CHUNK : 2 * CHUNK, :], sel)
        grad_log = dot_nn(tri_t, flows, highest) + extra[0:1, :]
        grad_dt = direct + rate * grad_log
        grad_raw = grad_dt * sigmoid(step_ref[chunk_rows(c), :].astype(f32) + bias)
        raw_ref[rows, :] = grad_raw.astype(bf16)
        gh_ref[0:1, :] += jnp.sum(grad_raw, axis=0, keepdims=True)
        gh_ref[1:2, :] += jnp.sum(grad_log * dt * rate, axis=0, keepdims=True)
        gh_ref[2:3, :] += extra[1:2, :]


def conv_back_kernel(
    act_ref, mixed_in_ref, ahead_ref, conv_ref, raw_ref, late_ref, rim_ref, cg_ref, gc_buf, mixed_ref
):
    block, wide = act_ref.shape
    chunks = block // CHUNK
    cg_ref[...] = jnp.zeros_like(cg_ref)
    gc_buf[0:8, :] = jnp.zeros((8, wide), f32)
    gc_buf[block + 8 :, :] = jnp.zeros((8, wide), f32)
    late_ref[:, wide:] = raw_ref[...]
    mixed_ref[0:HALO, :] = ahead_ref[...]
    mixed_ref[HALO:, :] = mixed_in_ref[...]

    @pl.loop(0, chunks)
    def _(i):
        c = chunks - 1 - i
        rows = chunk_rows(c)
        window = pl.ds(pl.multiple_of(c * CHUNK, 16), CHUNK + HALO)
        for n in range(0, wide, LANES):
            lanes = slice(n, n + LANES)
            win = mixed_ref[window, n : n + LANES].astype(f32)
            taps = [conv_ref[k : k + 1, lanes] for k in range(CONV)]
            moved = [win[HALO - 3 + k : HALO - 3 + k + CHUNK] for k in range(CONV)]
            conv = conv_ref[CONV : CONV + 1, lanes] + sum(t * m for t, m in zip(taps, moved))
            sig = sigmoid(conv)
            gc = act_ref[rows, lanes] * (sig * (1.0 + conv * (1.0 - sig)))
            gc_buf[pl.ds(pl.multiple_of(c * CHUNK + 8, 8), CHUNK), lanes] = gc
            for k in range(CONV):
                cg_ref[k : k + 1, lanes] += jnp.sum(gc * moved[k], axis=0, keepdims=True)
            cg_ref[CONV : CONV + 1, lanes] += jnp.sum(gc, axis=0, keepdims=True)
            span = gc_buf[pl.ds(pl.multiple_of(c * CHUNK + 8, 8), CHUNK + 8), lanes]
            late_ref[rows, lanes] = sum(
                taps[k] * span[CONV - 1 - k : CONV - 1 - k + CHUNK] for k in range(CONV)
            ).astype(bf16)

    row8 = lax.broadcasted_iota(jnp.int32, (8, LANES), 0)
    for n in range(0, wide, LANES):
        lanes = slice(n, n + LANES)
        span = gc_buf[0:24, lanes]
        rim = sum(conv_ref[k : k + 1, lanes] * span[8 - k : 16 - k] for k in range(CONV))
        rim_ref[:, lanes] = jnp.where(row8 < CONV - 1, rim, 0.0).astype(bf16)


def conv_back(act, mixed_in, ahead, conv_rows, raw):
    block, wide = act.shape
    return call(
        conv_back_kernel,
        (shape((block, wide + LANES), bf16), shape((8, wide), bf16), shape((8, wide), f32)),
        [VMEM] * 5,
        [pltpu.VMEM((block + 16, wide), f32), pltpu.VMEM((block + HALO, wide), bf16)],
        40 * block * wide * 16,
        act, mixed_in, ahead, conv_rows, raw,
    )


def scan_back(values, dy, keys, raw, dt, cum, starts, state_in, hp, packed):
    block, width = values.shape
    pairs, chunks = width // LANES, block // CHUNK
    return call(
        functools.partial(back_kernel, len(packed), pairs),
        (shape((block, width + KEYS), f32), shape((block, LANES), bf16), shape((8, LANES), f32)),
        [VMEM] * (9 + len(packed)),
        [
            pltpu.VMEM((STATE, width), f32),
            pltpu.VMEM((-(-chunks // 8) * 8, LANES), f32),
            pltpu.VMEM((2 * CHUNK, width), f32),
        ],
        40 * block * width * STATE,
        values, dy, keys, raw, dt, cum, starts, state_in, hp, *packed,
    )


def with_rim(late_ref, rim_ref, buffer):
    block = late_ref.shape[0]
    wide = rim_ref.shape[1]
    buffer[...] = late_ref[...]
    rim = jnp.concatenate([rim_ref[...].astype(f32), jnp.zeros((8, wide), f32)], axis=0)
    rim = pltpu.roll(rim, HALO - (CONV - 1), 0)
    last = late_ref[block - HALO :, 0:wide].astype(f32) + rim
    buffer[block - HALO :, 0:wide] = last.astype(bf16)


def late_kernel(plan_ref, normed_ref, late_ref, rim_ref, mine_ref, yours_ref, buffer):
    with_rim(late_ref, rim_ref, buffer)
    cols = late_ref.shape[1]
    owner = D // 8
    for side, ref in enumerate((mine_ref, yours_ref)):
        base = (plan_ref[CORE_AT] ^ side) * (D // 2)
        for g in range(0, D // 2, 2 * owner):
            at = pl.ds(pl.multiple_of(base + g, LANES), 2 * owner)
            for n in range(0, cols, 384):
                m = min(384, cols - n)
                grad = dot_tn(normed_ref[:, at], buffer[:, n : n + m]).astype(bf16)
                for r in range(0, 2 * owner, owner):
                    ref[(g + r) // owner, :, n : n + m] = grad[r : r + owner]


def late_products(plan, normed, late, rim):
    block, cols = late.shape
    return call(
        late_kernel,
        (shape((4, D // 8, cols), bf16),) * 2,
        [SMEM] + [VMEM] * 3,
        [pltpu.VMEM((block, cols), bf16)],
        2 * block * D * cols,
        plan, normed, late, rim,
    )


def place_vectors(plan_ref, cg_ref, gh_ref, go_ref, gg_ref, vec_ref):
    width = go_ref.shape[1]
    group = plan_ref[SEQ_AT]
    tiles = width // LANES
    heads = width // HEADDIM
    vec_ref[...] = jnp.zeros_like(vec_ref)
    for i in range(D // LANES):
        vec_ref[i : i + 1, :] = gg_ref[0:1, i * LANES : (i + 1) * LANES]
    at = D // LANES
    for k in range(CONV + 1):
        for i in range(tiles):
            vec_ref[pl.ds(at + tiles * group + i, 1), :] = cg_ref[k : k + 1, i * LANES : (i + 1) * LANES]
        for i in range(KEYS // LANES):
            low = width + i * LANES
            vec_ref[at + INNER // LANES + i : at + INNER // LANES + i + 1, :] = cg_ref[k : k + 1, low : low + LANES]
        at += CHANNELS // LANES
    for i in range(tiles):
        vec_ref[pl.ds(at + tiles * group + i, 1), :] = go_ref[0:1, i * LANES : (i + 1) * LANES]
    at += INNER // LANES
    lane = lax.broadcasted_iota(jnp.int32, (8, 2 * LANES), 1)
    own = jnp.concatenate([gh_ref[...], jnp.zeros((8, LANES), f32)], axis=1)
    own = jnp.where(lane < heads, own, 0.0)
    row = sum(pltpu.roll(own, HEADS * q + heads * group, 1)[q : q + 1] for q in range(3))
    vec_ref[at : at + 1, :] = row[:, :LANES]
    vec_ref[at + 1 : at + 2, :] = row[:, LANES:]


def input_kernel(
    n_w, w_at, placed, plan_ref, normed_ref, dg_ref, late_ref, rim_ref, gain_ref, cg_ref, gh_ref, go_ref, *refs
):
    w_refs = refs[:n_w]
    gi_ref, gg_ref, vec_ref, buffer, w_buf, sems = refs[n_w:]
    weights = Placer(w_refs, plan_ref, w_at, D // 16, w_buf, sems)
    weights.start()
    with_rim(late_ref, rim_ref, buffer)
    block, width = dg_ref.shape
    gg_ref[...] = jnp.zeros_like(gg_ref)
    weights.wait()
    tall = min(block, 512)
    for b in range(0, block, tall):
        for n in range(0, D, 256):
            lanes = slice(n, n + 256)
            grad = dot_nt(dg_ref[b : b + tall, :], w_buf[lanes, :width])
            grad = grad + dot_nt(buffer[b : b + tall, :], w_buf[lanes, width:])
            unit = normed_ref[b : b + tall, lanes].astype(f32) / gain_ref[:, lanes]
            gg_ref[0:1, lanes] += jnp.sum(grad * unit, axis=0, keepdims=True)
            gi_ref[b : b + tall, lanes] = grad.astype(bf16)
    if placed:
        place_vectors(plan_ref, cg_ref, gh_ref, go_ref, gg_ref, vec_ref)
    else:
        vec_ref[...] = jnp.zeros_like(vec_ref)


def input_products(plan, normed, grad_gate, late, rim, gain, conv_grads, head_grads, out_grads, weights, placed):
    block, cols = late.shape
    width = grad_gate.shape[1]
    n_w = len(weights[0])
    return call(
        functools.partial(input_kernel, n_w, weights[1], placed),
        (shape((block, D), bf16), shape((8, D), f32), shape((VEC_ROWS, LANES), f32)),
        [SMEM] + [VMEM] * 8 + [ANY] * n_w,
        [
            pltpu.VMEM((block, cols), bf16),
            pltpu.VMEM((D, width + cols), bf16),
            pltpu.SemaphoreType.DMA((n_w,)),
        ],
        2 * block * D * (cols + width),
        plan, normed, grad_gate, late, rim, gain, conv_grads, head_grads, out_grads, *weights[0],
    )


def adam_rates(step_count):
    step_float = step_count[0].astype(f32)
    corr_one = 1.0 - jnp.power(jnp.float32(beta_one), step_float)
    corr_two = 1.0 - jnp.power(jnp.float32(beta_two), step_float)
    return jnp.stack([1.0 / corr_one, 1.0 / corr_two])


def adam_math(weight, grad, moment, square, one, two):
    new_moment = beta_one * moment + (1.0 - beta_one) * grad
    new_square = beta_two * square + (1.0 - beta_two) * grad * grad
    update = -learn_rate * (
        new_moment * one / (jnp.sqrt(new_square * two) + adam_eps) + decay_rate * weight
    )
    return grad, new_moment, new_square, update


def adam_plain(weight, grad, moment, square, rates):
    return adam_math(weight.astype(f32), grad, moment, square, rates[0], rates[1])


def adam_in_kernel(n, width, heads, plan_ref, rate_ref, w_ref, m_ref, s_ref, *refs):
    early, late = refs[:n], refs[n : 2 * n]
    outs = refs[2 * n : 2 * n + 4]
    done, g = refs[2 * n + 4 :]
    done[...] = jnp.zeros_like(done)
    rows = w_ref.shape[0]
    keys_at, steps_at = 2 * INNER, 2 * INNER + KEYS
    g[:, keys_at:] = jnp.zeros((rows, g.shape[1] - keys_at), f32)
    lane = lax.broadcasted_iota(jnp.int32, (rows, LANES), 1)
    for i in range(n):

        @pl.when(plan_ref[LINE_AT + n + i] == 1)
        def _():
            place = plan_ref[LINE_AT + i]
            at = pl.multiple_of(place * width, LANES)
            g[:, pl.ds(at, width)] = early[i][...].astype(f32)
            g[:, pl.ds(INNER + at, width)] = late[i][:, 0:width].astype(f32)
            g[:, keys_at:steps_at] += late[i][:, width : width + KEYS].astype(f32)
            steps = jnp.where(lane < heads, late[i][:, width + KEYS :].astype(f32), 0.0)
            g[:, steps_at:] += pltpu.roll(steps, place * heads, 1)

    one, two = rate_ref[0], rate_ref[1]
    cols = w_ref.shape[1]
    for c in range(0, cols, 512):
        lanes = slice(c, min(c + 512, cols))
        results = adam_math(
            w_ref[:, lanes].astype(f32), g[:, lanes], m_ref[:, lanes], s_ref[:, lanes], one, two
        )
        for ref, value in zip(outs, results):
            ref[:, lanes] = value


def adam_in(plan, weight, moment, square, rates, early, late, width, heads):
    rows, cols = weight.shape
    tile = 32
    n = len(early[0])
    whole = pl.BlockSpec((tile, cols), lambda i: (i, 0))
    return pl.pallas_call(
        functools.partial(adam_in_kernel, n, width, heads),
        grid=(rows // tile,),
        out_shape=[shape((rows, cols), f32)] * 4 + [shape((8, LANES), f32)],
        in_specs=[SMEM, SMEM, whole, whole, whole]
        + [pl.BlockSpec((tile, a.shape[1]), lambda i: (i, 0)) for a in (*early[0], *late[0])],
        out_specs=[whole] * 4 + [pl.BlockSpec((8, LANES), lambda i: (0, 0))],
        scratch_shapes=[pltpu.VMEM((tile, 2 * INNER + KEYS + LANES), f32)],
        cost_estimate=pl.CostEstimate(flops=rows * cols * 20, bytes_accessed=rows * cols * 28, transcendentals=0),
        compiler_params=pltpu.CompilerParams(vmem_limit_bytes=48 * 1024 * 1024),
    )(plan, rates, weight, moment, square, *early[0], *late[0])


def adam_out_kernel(pos_ref, rate_ref, w_ref, m_ref, s_ref, *refs):
    pieces, outs = refs[:4], refs[4:8]
    done, g = refs[8:]
    done[...] = jnp.zeros_like(done)
    rows, cols = w_ref.shape
    width = pieces[0].shape[1]
    for k in range(4):

        @pl.when((pos_ref[0] ^ pl.program_id(0)) == k)
        def _():
            for half in range(cols // width):
                g[:, half * width : (half + 1) * width] = pieces[k][half * rows : (half + 1) * rows, :].astype(f32)

    one, two = rate_ref[0], rate_ref[1]
    for c in range(0, cols, 512):
        lanes = slice(c, min(c + 512, cols))
        results = adam_math(
            w_ref[:, lanes].astype(f32), g[:, lanes], m_ref[:, lanes], s_ref[:, lanes], one, two
        )
        for ref, value in zip(outs, results):
            ref[:, lanes] = value


def adam_out(weight, moment, square, rates, group, pieces):
    rows, cols = weight.shape
    tile = rows // 4
    whole = pl.BlockSpec((tile, cols), lambda i: (i, 0))
    return pl.pallas_call(
        adam_out_kernel,
        grid=(4,),
        out_shape=[shape((rows, cols), f32)] * 4 + [shape((8, LANES), f32)],
        in_specs=[SMEM, SMEM, whole, whole, whole] + [pl.BlockSpec(p.shape, lambda i: (0, 0)) for p in pieces],
        out_specs=[whole] * 4 + [pl.BlockSpec((8, LANES), lambda i: (0, 0))],
        scratch_shapes=[pltpu.VMEM((tile, cols), f32)],
        cost_estimate=pl.CostEstimate(flops=rows * cols * 20, bytes_accessed=rows * cols * 28, transcendentals=0),
        compiler_params=pltpu.CompilerParams(vmem_limit_bytes=48 * 1024 * 1024),
    )(group, rates, weight, moment, square, *pieces)


def pad_lanes(x, width):
    return x if x.shape[1] == width else jnp.pad(x, ((0, 0), (0, width - x.shape[1])))


def gather_all(tok, cot, local_in, out_weight, flat, width):
    me, me_c, me_d = lax.axis_index("seq"), lax.axis_index("ctx"), lax.axis_index("dp")
    vec_parts = [flat] + [lax.ppermute(flat, "ctx", flip_pairs(4, bit)) for bit in (1, 2, 3)]
    tok_near = line_near(tok)
    local_in = hold(local_in, vec_parts)
    w_x = lax.ppermute(local_in, "ctx", flip_pairs(4, 1))
    w_y = lax.ppermute(local_in, "ctx", flip_pairs(4, 2))
    w_d = lax.ppermute(local_in, "dp", CORES)
    cot_near = line_near(cot)
    vec_own = jnp.concatenate(hold(vec_parts, w_d), axis=0)
    vec_other = lax.ppermute(vec_own, "dp", CORES)
    tok_far = line_far(tok_near)
    half = local_in.shape[0] // 2
    w_up = lax.ppermute(w_y[:half], "ctx", flip_pairs(4, 1))
    w_down = lax.ppermute(w_x[half:], "ctx", flip_pairs(4, 2))
    w_xd = lax.ppermute(hold(w_x, vec_other), "dp", CORES)
    w_yd = lax.ppermute(hold(w_y, w_xd), "dp", CORES)
    first, second, third, fourth = out_row_pairs()
    beside = lax.ppermute(out_weight, WORLD, first)
    along = lax.ppermute(out_weight, WORLD, second)
    w_upd = lax.ppermute(hold(w_up, w_yd), "dp", CORES)
    w_downd = lax.ppermute(hold(w_down, w_upd), "dp", CORES)
    cot_far = line_far(cot_near)
    beyond = lax.ppermute(along, WORLD, third)
    source = (me_d == me // 2) & (me_c // 2 == lax.rem(me, 2))
    mine = jnp.where(source, out_weight, along)
    other = jnp.where(source, beside, beyond)
    mine_back = lax.ppermute(mine, WORLD, fourth)
    other_back = lax.ppermute(hold(other, mine_back), WORLD, fourth)
    out_rows = ((mine, other, mine_back, other_back), ROWS_AT)
    in_cols = ((local_in, w_x, w_y, w_up, w_down, w_d, w_xd, w_yd, w_upd, w_downd), COLS_AT)
    share_rows = flat.shape[0]
    vec = jnp.zeros((8, share_rows, LANES), flat.dtype)
    for d, rows in ((0, vec_own), (1, vec_other)):
        for c in range(4):
            block = rows[c * share_rows : (c + 1) * share_rows][None]
            vec = lax.dynamic_update_slice_in_dim(vec, block, (me_d ^ d) * 4 + (me_c ^ c), 0)
    return line_pieces(tok, tok_near, tok_far), line_pieces(cot, cot_near, cot_far), in_cols, out_rows, vec


def gather_all_plain(tok, cot, local_in, out_weight, flat, width):
    sidx = lax.axis_index("seq")
    tok_all = lax.all_gather(tok, "seq", axis=0, tiled=True)
    cot_all = lax.all_gather(cot, "seq", axis=0, tiled=True)
    in_cols = lax.all_gather(local_in, PLANE, axis=0, tiled=True)
    real = INNER // lax.axis_size("seq")
    out_rows = lax.dynamic_slice_in_dim(
        lax.all_gather(out_weight, PLANE, axis=0, tiled=True), sidx * real, real, 0
    )
    out_rows = jnp.pad(out_rows, ((0, width - real), (0, 0)))
    vec = lax.all_gather(flat, PLANE, axis=0, tiled=True).reshape(-1, *flat.shape)
    return ((tok_all,), 0), ((cot_all,), 0), ((in_cols,), 0), ((out_rows,), 0), vec


def per_device(
    tokens, cotangent, in_weight, out_weight, vectors, in_moment, in_square,
    out_moment, out_square, vec_moment, vec_square, step_count,
):
    seqs, sidx = lax.axis_size("seq"), lax.axis_index("seq")
    real, heads = INNER // seqs, HEADS // seqs
    width = -(-real // LANES) * LANES
    tok, cot = tokens[0], cotangent[0]
    block = tok.shape[0] * seqs
    by_hand = manual()
    plan = device_plan()

    share = vectors.shape[0]
    share_rows = -(-share // (LANES * 16)) * 16
    flat = jnp.pad(vectors, (0, share_rows * LANES - share)).reshape(share_rows, LANES)
    local_in = jnp.concatenate(
        [
            pad_lanes(lax.dynamic_slice_in_dim(in_weight, sidx * real, real, 1), width),
            pad_lanes(lax.dynamic_slice_in_dim(in_weight, INNER + sidx * real, real, 1), width),
            in_weight[:, 2 * INNER : 2 * INNER + KEYS],
            pad_lanes(lax.dynamic_slice_in_dim(in_weight, INNER + CHANNELS + sidx * heads, heads, 1), LANES),
        ],
        axis=1,
    )
    gather = gather_all if by_hand else gather_all_plain
    tok_parts, cot_parts, in_cols, out_rows, vec = gather(tok, cot, local_in, out_weight, flat, width)

    vec = vec.reshape(-1, share_rows * LANES)[:, :share].reshape(-1).astype(f32)
    offset = D
    gain_in = vec[:D][None]
    conv_weight = vec[offset : offset + (CONV + 1) * CHANNELS].reshape(CONV + 1, CHANNELS)
    offset += (CONV + 1) * CHANNELS
    gain_out = pad_lanes(lax.dynamic_slice_in_dim(vec[offset : offset + INNER], sidx * real, real)[None], width)
    offset += INNER
    head_rows = vec[offset:].reshape(3, HEADS)
    conv_rows = jnp.concatenate(
        [
            pad_lanes(lax.dynamic_slice_in_dim(conv_weight, sidx * real, real, 1), width),
            conv_weight[:, INNER:],
        ],
        axis=1,
    )
    conv_rows = jnp.pad(conv_rows, ((0, 3), (0, 0)))
    head_params = jnp.pad(
        lax.dynamic_slice_in_dim(head_rows, sidx * heads, heads, 1), ((0, 5), (0, LANES - heads))
    )

    if by_hand:
        gain_in = hold(gain_in, (conv_rows, head_params, gain_out))
    normed, gate, mixed_in, raw = project(plan, tok_parts, in_cols, gain_in, width, block)
    ahead = lax.ppermute(mixed_in[block - HALO :], "ctx", shift_pairs(lax.axis_size("ctx"), 1))
    values, keys, dt, cum, starts, packed = convolve(mixed_in, ahead, raw, conv_rows, head_params, width, block)
    sent = sent_states(packed, 1)
    y_inside = inside(values, keys, dt, cum, head_params)
    if by_hand:
        cot_arrays, out_arrays, y_inside = lax.optimization_barrier((cot_parts[0], out_rows[0], y_inside))
        cot_parts, out_rows = (cot_arrays, LINE_AT), (out_arrays, ROWS_AT)
    grad_normed = cot_product(plan, cot_parts, out_rows, width, block)
    mixed, sums, state_in = gate_forward(y_inside, grad_normed, keys, cum, starts, gate, gain_out, sent)
    if by_hand:
        all_sums = [sums] + [lax.ppermute(sums, "seq", flip_pairs(4, bit)) for bit in (3, 2, 1)]
    else:
        all_sums = [lax.psum(sums, "seq")]

    normed_out, grad_mixed, grad_gate, gain_out_grad, packed = norm_back(
        mixed, grad_normed, keys, cum, gate, gain_out, all_sums
    )
    sent = sent_states(packed, -1)
    early = early_products(plan, normed, normed_out, grad_gate, cot_parts, by_hand)
    part = out_product(plan, normed_out, out_rows).reshape(seqs, -1, D)
    if by_hand:
        early_chip = plane_reduce_core(*early)
        part_got = line_reduce_direct(part)
        early_got = plane_reduce_send(early_chip)

    grad_act, grad_raw, grad_heads = scan_back(
        values, grad_mixed, keys, raw, dt, cum, starts, state_in, head_params, sent
    )
    late, rim, conv_grads = conv_back(grad_act, mixed_in, ahead, conv_rows, grad_raw)
    rim = lax.ppermute(rim, "ctx", shift_pairs(lax.axis_size("ctx"), -1))
    if by_hand:
        early_mine = plane_reduced(early_chip, early_got)
        early_near = line_near(early_mine)

    in_late = late_products(plan, normed, late, rim)
    grad_in, gain_in_grad, vec_sum = input_products(
        plan, normed, grad_gate, late, rim, gain_in, conv_grads, grad_heads, gain_out_grad, in_cols, by_hand
    )
    grad_in = grad_in.reshape(seqs, -1, D)
    rates = adam_rates(step_count)
    in_rows = in_weight.shape[0]
    rank = lax.axis_index("dp") * lax.axis_size("ctx") + lax.axis_index("ctx")
    if by_hand:
        late_chip = plane_reduce_core(*in_late)
        late_got = plane_reduce_send(late_chip)
        early_near = hold(early_near, late_chip)
        early_far = line_far(early_near)
        early_pieces = line_pieces(early_mine, early_near, early_far)
        ordered = jnp.zeros((4, in_rows, width), bf16)
        me = sidx
        slots = [
            (me, early_mine),
            (lax.rem(me + 3, 4), jnp.where(me == 0, early_far[2], early_near[0])),
            (lax.rem(me + 1, 4), jnp.where(me == 3, early_far[2], early_near[1])),
            (lax.rem(me + 2, 4), jnp.where(me < 2, early_far[1], early_far[0])),
        ]
        for place, piece in slots:
            ordered = lax.dynamic_update_slice_in_dim(ordered, piece[in_rows:][None], place, 0)
        me_c = lax.axis_index("ctx")
        out_pieces = [
            lax.ppermute(lax.dynamic_index_in_dim(ordered, me_c ^ k, 0, False), WORLD, owner_pairs(k))
            for k in range(4)
        ]
        late_mine = plane_reduced(late_chip, late_got)
        late_near = line_near(late_mine)
        part_got = hold(part_got, late_near)
        block_sum = line_reduced(part, part_got)
        late_far = line_far(late_near)
        in_far = line_reduce_far(grad_in)
        late_pieces = line_pieces(late_mine, late_near, late_far)
        group = (rank // 2)[None].astype(jnp.int32)
        *out_out, _ = adam_out(out_weight, out_moment, out_square, rates, group, out_pieces)
        in_near = line_reduce_near(grad_in, hold(in_far, late_far))
        *in_out, in_done = adam_in(
            plan, in_weight, in_moment, in_square, rates, early_pieces, late_pieces, width, heads
        )
        input_sum = line_reduced(grad_in, hold(in_near, in_done))
    else:
        block_sum = lax.psum_scatter(part, "seq", scatter_dimension=0).astype(f32)
        input_sum = lax.psum_scatter(grad_in, "seq", scatter_dimension=0).astype(f32)
        core = lax.axis_index("dp")
        ordered = jnp.concatenate(
            [jnp.where(core == 0, in_late[0], in_late[1]), jnp.where(core == 0, in_late[1], in_late[0])], axis=0
        )
        grads = jnp.concatenate([early[0].reshape(8, in_rows, width), ordered], axis=2)
        grads = lax.psum_scatter(grads, PLANE, scatter_dimension=0)
        grads = lax.all_gather(grads, "seq").astype(f32)
        steps_at = 2 * width + KEYS
        in_total = jnp.concatenate(
            [grads[s, :, :real] for s in range(seqs)]
            + [grads[s, :, width : width + real] for s in range(seqs)]
            + [jnp.sum(grads[:, :, 2 * width : steps_at], axis=0)]
            + [grads[s, :, steps_at : steps_at + heads] for s in range(seqs)],
            axis=1,
        )
        out_cols = early[1][:real].reshape(real, 8, D // 8).transpose(1, 0, 2)
        out_cols = lax.psum_scatter(out_cols, PLANE, scatter_dimension=0)
        out_cols = lax.all_gather(out_cols, "seq", axis=0, tiled=True)
        out_total = lax.all_to_all(out_cols, PLANE, split_axis=0, concat_axis=1, tiled=True).astype(f32)
        in_out = adam_plain(in_weight, in_total, in_moment, in_square, rates)
        out_out = adam_plain(out_weight, out_total, out_moment, out_square, rates)

    block_out = (tok.astype(f32) + block_sum).astype(bf16)
    grad_unit = input_sum * gain_in
    own = tok.astype(f32)
    scale = lax.rsqrt(jnp.mean(own * own, axis=1, keepdims=True) + eps_norm)
    unit = own * scale
    token_grad = cot.astype(f32) + scale * (grad_unit - unit * jnp.mean(grad_unit * unit, axis=1, keepdims=True))

    if not by_hand:
        conv_place = jnp.concatenate(
            [
                lax.dynamic_update_slice_in_dim(
                    jnp.zeros((CONV + 1, INNER), f32), conv_grads[: CONV + 1, :real], sidx * real, 1
                ),
                conv_grads[: CONV + 1, width:],
            ],
            axis=1,
        )
        gain_place = lax.dynamic_update_slice_in_dim(
            jnp.zeros((INNER,), f32), gain_out_grad[0, :real], sidx * real, 0
        )
        head_place = lax.dynamic_update_slice_in_dim(
            jnp.zeros((3, HEADS), f32), grad_heads[:3, :heads], sidx * heads, 1
        )
        vec_local = jnp.concatenate([gain_in_grad[0], conv_place.reshape(-1), gain_place, head_place.reshape(-1)])
        length = vec_local.shape[0]
        vec_rows = -(-length // (LANES * 8)) * 8
        vec_sum = jnp.pad(vec_local, (0, vec_rows * LANES - length)).reshape(vec_rows, LANES)
    for axis in ("dp", "ctx", "seq"):
        if by_hand and axis != "dp":
            vec_sum = hold(vec_sum, late_mine if axis == "ctx" else (part_got, late_far))
        vec_sum = total_over(vec_sum, axis, in_done if by_hand and axis == "seq" else None)
    vec_total = lax.dynamic_slice_in_dim(vec_sum.reshape(-1), rank * share, share)
    vec_out = adam_plain(vectors, vec_total, vec_moment, vec_square, rates)
    return (block_out[None], token_grad[None], *in_out, *out_out, *vec_out)


def solution(mesh):
    rows, weights, vector = P("dp", ("ctx", "seq"), None), P(PLANE, None), P(PLANE)
    in_specs = (
        rows, rows, weights, weights, vector, weights, weights, weights, weights, vector, vector, P(),
    )
    out_specs = (rows, rows) + (weights,) * 8 + (vector,) * 4
    mapped = jax.shard_map(per_device, mesh=mesh, in_specs=in_specs, out_specs=out_specs, check_vma=False)
    if dict(mesh.shape) == {"dp": 2, "ctx": 4, "seq": 4}:
        return mapped
    return mapped
```
